32 devices in a mesh: tm: 4 (over z), grid: 8 (over y, x, core).
Axes of the slice: x: 2, y: 2, z: 4, core: 2. Of those that a mesh axis runs over, the one named last changes fastest.
Arguments:
- starts: float32 [4, 3, 1024, 1024], P('tm', None, 'grid'), may hold values from -1.6 to 1.6
- coriolis: float32 [1024], P('grid'), may hold values from 100 to 800
Outputs:
- ends: float32 [4, 3, 1024, 1024], P('tm', None, 'grid')
The draws below stay inside these ranges and needn't reach their ends.
All inputs are finite; a program needn't handle non-finite values.
Results may differ from the reference program's by a relative error of at most 0.0003.
Values sent between devices are 32-bit elements; how exact they have to be, the bound alone decides.
No kernel may reach another device: no remote copies, remote signals or barrier semaphores. Data moves between devices by JAX's collectives and lax.ppermute only.
A program may use at most 128 MiB of HBM per device.

```python
import math
import jax
import jax.numpy as jnp
from jax import lax

NX = 1024
SWEEPS = 2
SLICES = 4


def block_scale(key, dims, split, low, largest):
    factor_of, own = 1.0, jax.random.fold_in(key, 6)
    for axis_at, shards_of in split:
        heights = jnp.exp(jax.random.uniform(jax.random.fold_in(own, axis_at), (shards_of,), jnp.float32, low / len(split), largest / len(split)))
        factor_of = factor_of * jnp.repeat(heights, dims[axis_at] // shards_of).reshape([-1 if axis == axis_at else 1 for axis in range(len(dims))])
    return factor_of


def scatter_about(rng, dims, deviation, limit, split=(), kind=jnp.bfloat16):
    factor_of = block_scale(rng, dims, split, -0.22, 0.18) if split else 1.0
    values = jax.random.normal(rng, dims, jnp.float32) * deviation * factor_of
    return jnp.minimum(jnp.maximum(values, -limit), limit).astype(kind)


def setup_inputs(seed: int = 0) -> dict:
    streams_of = jax.random.split(jax.random.key(seed), 3)
    starts = scatter_about(streams_of[0], (SLICES, 3, NX, NX), 0.4, 1.6, ((0, 4), (2, 8)), jnp.float32)
    coriolis = jnp.clip(jnp.exp(math.log(800.0) - 2.0794415 * jax.random.uniform(streams_of[1], (NX,), jnp.float32) ** block_scale(streams_of[1], (NX,), ((0, 8),), -0.2, 0.2)), 100.0, 800.0)
    return {"starts": starts, "coriolis": coriolis}


STEP_LENGTH = 1e-3
GRAVITY = 1.0
WEIGHTS_FIRST = (5.0 / 24.0, 8.0 / 24.0, -1.0 / 24.0)
WEIGHTS_SECOND = (-1.0 / 24.0, 8.0 / 24.0, 5.0 / 24.0)


def wavenumbers(length):
    counter = jnp.arange(length, dtype=jnp.int32)
    signed = jnp.where(counter < length // 2, counter, counter - length)
    signed = jnp.where(counter == length // 2, 0, signed)
    return signed.astype(jnp.float32)


def along_x(values):
    waves = wavenumbers(values.shape[-1])
    spectrum = jnp.fft.fft(values, axis=-1)
    return jnp.real(jnp.fft.ifft(1j * waves * spectrum, axis=-1)).astype(values.dtype)


def along_y(values):
    waves = wavenumbers(values.shape[-2])[:, None]
    spectrum = jnp.fft.fft(values, axis=-2)
    return jnp.real(jnp.fft.ifft(1j * waves * spectrum, axis=-2)).astype(values.dtype)


def tendency(state_now, coriolis):
    height, east_vel, north_vel = state_now[0], state_now[1], state_now[2]
    turning = coriolis[:, None]
    height_x = along_x(height)
    height_y = along_y(height)
    east_x = along_x(east_vel)
    east_y = along_y(east_vel)
    north_x = along_x(north_vel)
    north_y = along_y(north_vel)
    rate_height = -(east_vel * height_x + north_vel * height_y) - (1.0 + height) * (east_x + north_y)
    rate_east = -(east_vel * east_x + north_vel * east_y) + turning * north_vel - GRAVITY * height_x
    rate_north = -(east_vel * north_x + north_vel * north_y) - turning * east_vel - GRAVITY * height_y
    return jnp.stack([rate_height, rate_east, rate_north])


def quadrature(weights, rates):
    return weights[0] * rates[0] + weights[1] * rates[1] + weights[2] * rates[2]


def reference(starts, coriolis):
    def rates_of(states):
        return lax.map(lambda single: tendency(single, coriolis), states)

    first_rates = rates_of(starts)
    old_nodes = (starts, starts, starts)
    old_rates = (first_rates, first_rates, first_rates)
    for sweep_index in range(SWEEPS):
        node_zero = jnp.concatenate([starts[:1], old_nodes[2][:-1]], axis=0)
        rate_zero = rates_of(node_zero)
        node_one = node_zero + 0.5 * STEP_LENGTH * (rate_zero - old_rates[0]) + STEP_LENGTH * quadrature(WEIGHTS_FIRST, old_rates)
        rate_one = rates_of(node_one)
        node_two = node_one + 0.5 * STEP_LENGTH * (rate_one - old_rates[1]) + STEP_LENGTH * quadrature(WEIGHTS_SECOND, old_rates)
        if sweep_index + 1 < SWEEPS:
            rate_two = rates_of(node_two)
        else:
            rate_two = old_rates[2]
        old_nodes = (node_zero, node_one, node_two)
        old_rates = (rate_zero, rate_one, rate_two)
    return old_nodes[2]
```

```python
import functools
import math

import jax
import jax.numpy as jnp
import ml_dtypes
import numpy as np
from jax import lax
from jax.experimental import pallas as pl
from jax.experimental.pallas import tpu as pltpu
from jax.sharding import PartitionSpec as P

SWEEPS = 2
STEP_LENGTH = 0.001
HALF_STEP = 0.5 * STEP_LENGTH
GRAVITY = 1.0
CORRECT_FIRST = (5.0 / 24.0 - 0.5, 8.0 / 24.0, -1.0 / 24.0)
CORRECT_SECOND = (-1.0 / 24.0, 8.0 / 24.0 - 0.5, 5.0 / 24.0)
TOLERANCE = 1e-8
TILE = 256
ROWS = 16
F32 = jnp.float32
BF16 = jnp.bfloat16


def kernel_values(length):
    values = np.zeros(length)
    for j in range(1, length):
        values[j] = (0.5 if j % 2 == 0 else -0.5) / math.tan(math.pi * j / length)
    values[length // 2] = 0.0
    return values


def toeplitz(values, rows, cols, offset):
    index = np.arange(rows)[:, None] - np.arange(cols)[None, :] + offset
    return values[index % len(values)]


def cross_factors(block, tolerance):
    rest = block.copy()
    lefts, rights = [], []
    while True:
        at = int(np.argmax(np.abs(rest)))
        i, j = divmod(at, rest.shape[1])
        pivot = rest[i, j]
        small = abs(pivot) <= tolerance
        if (small and lefts and len(lefts) % 8 == 0) or len(lefts) == block.shape[0]:
            break
        if abs(pivot) == 0.0:
            left, right = np.zeros(rest.shape[0]), np.zeros(rest.shape[1])
        else:
            left, right = rest[:, j] / pivot, rest[i, :].copy()
        lefts.append(left)
        rights.append(right)
        rest = rest - left[:, None] * right[None, :]
    return np.stack(lefts, axis=1), np.stack(rights, axis=0)


def two_parts(table):
    high = table.astype(ml_dtypes.bfloat16)
    low = (table - high.astype(np.float64)).astype(ml_dtypes.bfloat16)
    return high, low


def pad_rows(table, multiple):
    extra = -table.shape[0] % multiple
    return np.pad(table, ((0, extra), (0, 0)))


def x_tables(length):
    values = kernel_values(length)
    half = length // 2
    near = toeplitz(values, half, half, 0).T
    far = toeplitz(values, half, half, half).T
    plus = two_parts(0.5 * (near + far))
    minus = two_parts(0.5 * (near - far))
    return np.stack([plus[0], plus[1], minus[0], minus[1]])


@functools.lru_cache(maxsize=None)
def y_tables(length, devices):
    rows = length // devices
    pair = 2 * rows
    pairs = devices // 2
    values = kernel_values(length)
    tolerance = TOLERANCE * float(np.max(np.abs(values)))
    factors = [cross_factors(toeplitz(values, pair, pair, d * pair), tolerance) for d in range(1, pairs)]
    ranks = tuple(f[0].shape[1] for f in factors)
    mates = [cross_factors(toeplitz(values, rows, rows, rows if k == 0 else -rows), tolerance) for k in range(2)]
    mate_rank = max(m[0].shape[1] for m in mates)
    send, apply = [], []
    for k in range(2):
        span = slice(k * rows, (k + 1) * rows)
        to_mate = np.pad(mates[k][1], ((0, mate_rank - mates[k][1].shape[0]), (0, 0)))
        from_mate = np.pad(mates[1 - k][0], ((0, 0), (0, mate_rank - mates[1 - k][0].shape[1])))
        down = pad_rows(np.concatenate([f[1][:, span] for f in factors] + [to_mate], axis=0), 16)
        send.append(np.concatenate(two_parts(down), axis=0))
        own = pad_rows(toeplitz(values, rows, rows, 0).T, 16).T
        up = np.concatenate([own] + [f[0][span] for f in factors] + [from_mate], axis=1)
        up = pad_rows(up.T, 16).T
        apply.append(np.concatenate(two_parts(up), axis=0))
    return ranks, mate_rank, np.stack(send), np.stack(apply)


def parts_of(value):
    high = value.astype(BF16)
    return high, (value - high.astype(F32)).astype(BF16)


def dot(left, right):
    return jnp.dot(left, right, preferred_element_type=F32)


def product(stacked, high, low):
    count = stacked.shape[0] // 2
    both = dot(stacked, high)
    return both[:count] + both[count:] + dot(stacked[:count], low)


def x_kernel(state_ref, table_ref, out_ref):
    value = state_ref[...]
    half = value.shape[1] // 2
    left, right = value[:, :half], value[:, half:]

    def folded(total, at):
        high, low = parts_of(total)
        return dot(high, table_ref[at]) + dot(low, table_ref[at]) + dot(high, table_ref[at + 1])

    even = folded(left + right, 0)
    odd = folded(left - right, 2)
    out_ref[:, :half] = even + odd
    out_ref[:, half:] = even - odd


def along_x(state, table):
    fields, rows, length = state.shape
    out = pl.pallas_call(
        x_kernel,
        grid=(fields,),
        in_specs=[
            pl.BlockSpec((rows, length), lambda f: (f, 0)),
            pl.BlockSpec(table.shape, lambda f: (0, 0, 0)),
        ],
        out_specs=pl.BlockSpec((rows, length), lambda f: (f, 0)),
        out_shape=jax.ShapeDtypeStruct((fields * rows, length), F32),
        name="along_x",
    )(state.reshape(fields * rows, length), table)
    return out.reshape(state.shape)


class Plan:
    def __init__(self, rows, length, ranks, mate_rank):
        self.rows, self.length = rows, length
        self.ranks, self.mate_rank = ranks, mate_rank
        self.total = sum(ranks)
        self.half = length // 2
        self.per_half = self.half // TILE
        self.tiles = length // TILE
        self.state = jax.ShapeDtypeStruct((3, rows, length), F32)
        self.state_spec = pl.BlockSpec((3, rows, TILE), lambda t, flags: (0, 0, t))
        self.row_blocks = [(r, min(ROWS, rows - r)) for r in range(0, rows, ROWS)]

    def whole(self, shape):
        return pl.BlockSpec(shape, lambda t, flags: (0,) * len(shape))

    def moment_outs(self):
        half = jax.ShapeDtypeStruct((3, self.total, self.half), F32)
        mate = jax.ShapeDtypeStruct((3, self.mate_rank, self.length), F32)
        return (half, half, mate), (
            self.whole(half.shape),
            self.whole(half.shape),
            pl.BlockSpec((3, self.mate_rank, TILE), lambda t, flags: (0, 0, t)),
        )

    def emit_moments(self, flags_ref, next_ref, send_ref, mine_ref, theirs_ref, mate_ref):
        tile = pl.program_id(0)
        is_mine = tile // self.per_half == flags_ref[0]
        start = pl.multiple_of((tile % self.per_half) * TILE, TILE)
        for f in range(3):
            found = product(send_ref[...], *parts_of(next_ref[f]))
            mate_ref[f] = found[self.total : self.total + self.mate_rank]

            @pl.when(is_mine)
            def _():
                mine_ref[f, :, pl.ds(start, TILE)] = found[: self.total]

            @pl.when(jnp.logical_not(is_mine))
            def _():
                theirs_ref[f, :, pl.ds(start, TILE)] = found[: self.total]

    def y_gradient(self, f, flags_ref, state_ref, mine_refs, other_refs, mate_ref, apply_ref):
        tile = pl.program_id(0)
        is_mine = tile // self.per_half == flags_ref[0]
        start = pl.multiple_of((tile % self.per_half) * TILE, TILE)
        pieces = [state_ref[f]]
        if self.rows % 16:
            pieces.append(jnp.zeros((-self.rows % 16, TILE), F32))
        for a, b in zip(mine_refs, other_refs):
            here = a[f, :, pl.ds(start, TILE)]
            there = b[f, :, pl.ds(start, TILE)]
            pieces.append(jnp.where(is_mine, here, there))
        pieces.append(mate_ref[f])
        width = apply_ref.shape[1] - sum(p.shape[0] for p in pieces)
        if width:
            pieces.append(jnp.zeros((width, TILE), F32))
        return product(apply_ref[...], *parts_of(jnp.concatenate(pieces, axis=0)))


def tendency_rows(h, u, v, gx, gy, turning):
    rate_h = -(u * gx[0] + v * gy[0]) - (1.0 + h) * (gx[1] + gy[2])
    rate_u = -(u * gx[1] + v * gy[1]) + turning * v - GRAVITY * gx[0]
    rate_v = -(u * gx[2] + v * gy[2]) - turning * u - GRAVITY * gy[0]
    return rate_h, rate_u, rate_v


def select_call(plan, flags, received, own, added, send):
    extra = [] if added is None else [added]

    def body(flags_ref, received_ref, own_ref, *rest):
        added_ref = rest[0] if extra else None
        send_ref, next_ref, mine_ref, theirs_ref, mate_ref = rest[len(extra) :]
        first = flags_ref[1] == 0
        for f in range(3):
            value = jnp.where(first, own_ref[f], received_ref[f])
            next_ref[f] = value if added_ref is None else value + added_ref[f]
        plan.emit_moments(flags_ref, next_ref, send_ref, mine_ref, theirs_ref, mate_ref)

    shapes, specs = plan.moment_outs()
    return pl.pallas_call(
        body,
        grid_spec=pltpu.PrefetchScalarGridSpec(
            num_scalar_prefetch=1,
            grid=(plan.tiles,),
            in_specs=[plan.state_spec] * (2 + len(extra)) + [plan.whole(send.shape)],
            out_specs=[plan.state_spec, *specs],
        ),
        out_shape=[plan.state, *shapes],
        name="select_state",
    )(flags, received, own, *extra, send)


def stage_call(plan, flags, stage, state, grad_x, received, turning, apply, send, others):
    mine, other, mate = received
    count = len(mine)
    with_moments = stage in (1, 2)

    def body(flags_ref, state_ref, grad_ref, turning_ref, *rest):
        mine_refs, rest = rest[:count], rest[count:]
        other_refs, rest = rest[:count], rest[count:]
        mate_ref, apply_ref, rest = rest[0], rest[1], rest[2:]
        other_ins, rest = rest[: len(others)], rest[len(others) :]
        if with_moments:
            send_ref, rest = rest[0], rest[1:]
        grad_y = rest[-1]
        for f in range(3):
            grad_y[f] = plan.y_gradient(f, flags_ref, state_ref, mine_refs, other_refs, mate_ref, apply_ref)
        for start, size in plan.row_blocks:
            at = slice(start, start + size)
            now = [state_ref[f, at, :] for f in range(3)]
            rates = tendency_rows(
                *now,
                [grad_ref[f, at, :] for f in range(3)],
                [grad_y[f, at, :] for f in range(3)],
                turning_ref[at, :],
            )
            for f in range(3):
                ahead = now[f] + HALF_STEP * rates[f]
                if stage in (1, 2):
                    rest[0][f, at, :] = ahead
                    rest[1][f, at, :] = rates[f]
                elif stage == 3:
                    rest[0][f, at, :] = ahead
                    olds = (other_ins[0][f, at, :], other_ins[1][f, at, :], rates[f])
                    for out, weights in ((rest[1], CORRECT_FIRST), (rest[2], CORRECT_SECOND)):
                        out[f, at, :] = sum((STEP_LENGTH * w) * r for w, r in zip(weights, olds))
                else:
                    rest[0][f, at, :] = ahead + other_ins[0][f, at, :]
        if with_moments:
            plan.emit_moments(flags_ref, rest[0], send_ref, *rest[2:5])

    state_outs = {1: 2, 2: 2, 3: 3, 4: 1}[stage]
    shapes, specs = plan.moment_outs() if with_moments else ((), ())
    mate_spec = pl.BlockSpec((3, plan.mate_rank, TILE), lambda t, flags: (0, 0, t))
    return pl.pallas_call(
        body,
        grid_spec=pltpu.PrefetchScalarGridSpec(
            num_scalar_prefetch=1,
            grid=(plan.tiles,),
            in_specs=[plan.state_spec] * 2
            + [plan.whole(turning.shape)]
            + [plan.whole(a.shape) for a in (*mine, *other)]
            + [mate_spec, plan.whole(apply.shape)]
            + [plan.state_spec] * len(others)
            + ([plan.whole(send.shape)] if with_moments else []),
            out_specs=[plan.state_spec] * state_outs + list(specs),
            scratch_shapes=[pltpu.VMEM((3, plan.rows, TILE), F32)],
        ),
        out_shape=[plan.state] * state_outs + list(shapes),
        name=f"stage_{stage}",
    )(flags, state, grad_x, turning, *mine, *other, mate, apply, *others, *([send] if with_moments else []))


def ahead_in_time(array):
    size = lax.axis_size("tm")
    return lax.ppermute(array, "tm", [(i, i + 1) for i in range(size - 1)])


def mate_swap(array):
    size = lax.axis_size("grid")
    return lax.ppermute(array, "grid", [(i, i ^ 1) for i in range(size)])


def exchange(plan, mine, theirs, to_mate):
    size = lax.axis_size("grid")
    from_mate = mate_swap(to_mate)
    merged = mine + mate_swap(theirs)
    mine_in, other_in, start = [], [], 0
    for d, rank in enumerate(plan.ranks, 1):
        part = merged[:, start : start + rank]
        start += rank
        mine_in.append(lax.ppermute(part, "grid", [(i, (i + 2 * d) % size) for i in range(size)]))
    for part in mine_in:
        other_in.append(mate_swap(part))
    return mine_in, other_in, from_mate


def per_device(starts, coriolis):
    first_state = starts[0]
    _, rows, length = first_state.shape
    ranks, mate_rank, send_tables, apply_tables = y_tables(length, lax.axis_size("grid"))
    plan = Plan(rows, length, ranks, mate_rank)
    member = lax.axis_index("grid") % 2
    flags = jnp.stack([member, lax.axis_index("tm")]).astype(jnp.int32)
    table = jnp.asarray(x_tables(length))
    send = lax.dynamic_index_in_dim(jnp.asarray(send_tables), member, 0, keepdims=False)
    apply = lax.dynamic_index_in_dim(jnp.asarray(apply_tables), member, 0, keepdims=False)
    turning = coriolis[:, None]

    def stage(number, state, moments, others=()):
        received = exchange(plan, *moments)
        grad_x = along_x(state, table)
        return stage_call(plan, flags, number, state, grad_x, received, turning, apply, send, others)

    before = ahead_in_time(first_state)
    node_zero, *moments = select_call(plan, flags, before, first_state, None, send)
    node_one, rate_zero, *moments = stage(1, node_zero, moments)
    node_two, rate_one, *moments = stage(2, node_one, moments)
    lead, add_first, add_second = stage(3, node_two, moments, (rate_zero, rate_one))
    came = ahead_in_time(lead)
    node, *moments = select_call(plan, flags, came, node_one, add_first, send)
    (ends,) = stage(4, node, moments, (add_second,))
    return ends[None]


def solution(mesh):
    return jax.shard_map(
        per_device,
        mesh=mesh,
        in_specs=(P("tm", None, "grid", None), P("grid")),
        out_specs=P("tm", None, "grid", None),
        check_vma=False,
    )
```

```python
import functools
import math

import jax
import jax.numpy as jnp
import ml_dtypes
import numpy as np
from jax import lax
from jax.experimental import pallas as pl
from jax.experimental.pallas import tpu as pltpu
from jax.sharding import PartitionSpec as P

SWEEPS = 2
STEP_LENGTH = 0.001
HALF_STEP = 0.5 * STEP_LENGTH
GRAVITY = 1.0
CORRECT_FIRST = (5.0 / 24.0 - 0.5, 8.0 / 24.0, -1.0 / 24.0)
CORRECT_SECOND = (-1.0 / 24.0, 8.0 / 24.0 - 0.5, 5.0 / 24.0)
TOLERANCE = 1e-8
ROWS = 8
KERNEL_BYTES = 20 * 2**20
F32 = jnp.float32
BF16 = jnp.bfloat16


def kernel_values(length):
    values = np.zeros(length)
    for j in range(1, length):
        values[j] = (0.5 if j % 2 == 0 else -0.5) / math.tan(math.pi * j / length)
    values[length // 2] = 0.0
    return values


def toeplitz(values, rows, cols, offset):
    index = np.arange(rows)[:, None] - np.arange(cols)[None, :] + offset
    return values[index % len(values)]


def cross_factors(block, tolerance):
    rest = block.copy()
    lefts, rights = [], []
    while True:
        at = int(np.argmax(np.abs(rest)))
        i, j = divmod(at, rest.shape[1])
        pivot = rest[i, j]
        small = abs(pivot) <= tolerance
        if (small and lefts and len(lefts) % 8 == 0) or len(lefts) == block.shape[0]:
            break
        if abs(pivot) == 0.0:
            left, right = np.zeros(rest.shape[0]), np.zeros(rest.shape[1])
        else:
            left, right = rest[:, j] / pivot, rest[i, :].copy()
        lefts.append(left)
        rights.append(right)
        rest = rest - left[:, None] * right[None, :]
    return np.stack(lefts, axis=1), np.stack(rights, axis=0)


def two_parts(table):
    high = table.astype(ml_dtypes.bfloat16)
    low = (table - high.astype(np.float64)).astype(ml_dtypes.bfloat16)
    return high, low


def pad_rows(table, multiple):
    extra = -table.shape[0] % multiple
    return np.pad(table, ((0, extra), (0, 0)))


def x_tables(length):
    values = kernel_values(length)
    half = length // 2
    near = toeplitz(values, half, half, 0).T
    far = toeplitz(values, half, half, half).T
    plus = two_parts(0.5 * (near + far))
    minus = two_parts(0.5 * (near - far))
    return np.stack([plus[0], plus[1], minus[0], minus[1]])


@functools.lru_cache(maxsize=None)
def y_tables(length, devices):
    rows = length // devices
    pair = 2 * rows
    pairs = devices // 2
    values = kernel_values(length)
    tolerance = TOLERANCE * float(np.max(np.abs(values)))
    factors = [cross_factors(toeplitz(values, pair, pair, d * pair), tolerance) for d in range(1, pairs)]
    ranks = tuple(f[0].shape[1] for f in factors)
    mates = [cross_factors(toeplitz(values, rows, rows, rows if k == 0 else -rows), tolerance) for k in range(2)]
    mate_rank = max(m[0].shape[1] for m in mates)
    send, apply = [], []
    for k in range(2):
        span = slice(k * rows, (k + 1) * rows)
        to_mate = np.pad(mates[k][1], ((0, mate_rank - mates[k][1].shape[0]), (0, 0)))
        from_mate = np.pad(mates[1 - k][0], ((0, 0), (0, mate_rank - mates[1 - k][0].shape[1])))
        down = pad_rows(np.concatenate([f[1][:, span] for f in factors] + [to_mate], axis=0), 16)
        send.append(np.concatenate(two_parts(down), axis=0))
        own = pad_rows(toeplitz(values, rows, rows, 0).T, 16).T
        up = np.concatenate([own] + [f[0][span] for f in factors] + [from_mate], axis=1)
        up = pad_rows(up.T, 16).T
        apply.append(np.concatenate(two_parts(up), axis=0))
    return ranks, mate_rank, np.stack(send), np.stack(apply)


def parts_of(value):
    high = value.astype(BF16)
    return high, (value - high.astype(F32)).astype(BF16)


def dot(left, right):
    return jnp.dot(left, right, preferred_element_type=F32)


def product(stacked, high, low):
    count = stacked.shape[0] // 2
    both = dot(stacked, high)
    return both[:count] + both[count:] + dot(stacked[:count], low)


VMEM = pl.BlockSpec(memory_space=pltpu.VMEM)
SMEM = pl.BlockSpec(memory_space=pltpu.SMEM)


def on_chip_call(body, operands, shapes, scalars=1, keep=True, **options):
    held = [pltpu.with_memory_space_constraint(a, pltpu.VMEM) for a in operands[scalars:]]
    outs = [pltpu.VMEM(s.shape, s.dtype) for s in shapes] if keep else shapes
    return pl.pallas_call(
        body,
        in_specs=[SMEM] * scalars + [VMEM] * len(held),
        out_specs=[VMEM] * len(outs),
        out_shape=outs,
        compiler_params=pltpu.CompilerParams(vmem_limit_bytes=KERNEL_BYTES),
        **options,
    )(*operands[:scalars], *held)


def x_kernel(state_ref, table_ref, out_ref):
    half = state_ref.shape[1] // 2
    left, right = state_ref[:, :half], state_ref[:, half:]

    def folded(total, at):
        high, low = parts_of(total)
        return dot(high, table_ref[at]) + dot(low, table_ref[at]) + dot(high, table_ref[at + 1])

    even = folded(left + right, 0)
    odd = folded(left - right, 2)
    out_ref[:, :half] = even + odd
    out_ref[:, half:] = even - odd


def along_x(state, table):
    fields, rows, length = state.shape
    flat = state.reshape(fields * rows, length)
    cost = pl.CostEstimate(
        flops=6 * flat.shape[0] * length * length // 2,
        transcendentals=0,
        bytes_accessed=8 * flat.size + 2 * table.size,
    )
    shape = jax.ShapeDtypeStruct(flat.shape, F32)
    (out,) = on_chip_call(x_kernel, [flat, table], [shape], scalars=0, cost_estimate=cost, name="along_x")
    return out.reshape(state.shape)


class Plan:
    def __init__(self, rows, length, ranks, mate_rank):
        self.rows, self.length = rows, length
        self.ranks, self.mate_rank = ranks, mate_rank
        self.total = sum(ranks)
        self.half = length // 2
        self.state = jax.ShapeDtypeStruct((3, rows, length), F32)
        half = jax.ShapeDtypeStruct((3, self.total, self.half), F32)
        self.moments = (half, half, jax.ShapeDtypeStruct((3, mate_rank, length), F32))

    def halves(self, flags_ref):
        member = flags_ref[0]
        for slot, at in ((0, member), (1, 1 - member)):
            yield slot, pl.ds(pl.multiple_of(at * self.half, 128), self.half)

    def emit_moments(self, slot, cols, next_ref, send_ref, moment_refs):
        for f in range(3):
            found = product(send_ref[...], *parts_of(next_ref[f, :, cols]))
            moment_refs[slot][f] = found[: self.total]
            moment_refs[2][f, :, cols] = found[self.total : self.total + self.mate_rank]

    def y_gradient(self, f, cols, state_ref, pair_refs, mate_ref, apply_ref):
        pieces = [state_ref[f, :, cols]]
        if self.rows % 16:
            pieces.append(jnp.zeros((-self.rows % 16, self.half), F32))
        pieces += [ref[f] for ref in pair_refs]
        pieces.append(mate_ref[f, :, cols])
        width = apply_ref.shape[1] - sum(p.shape[0] for p in pieces)
        if width:
            pieces.append(jnp.zeros((width, self.half), F32))
        return product(apply_ref[...], *parts_of(jnp.concatenate(pieces, axis=0)))


def tendency_rows(h, u, v, gx, gy, turning):
    rate_h = -(u * gx[0] + v * gy[0]) - (1.0 + h) * (gx[1] + gy[2])
    rate_u = -(u * gx[1] + v * gy[1]) + turning * v - GRAVITY * gx[0]
    rate_v = -(u * gx[2] + v * gy[2]) - turning * u - GRAVITY * gy[0]
    return rate_h, rate_u, rate_v


def select_call(plan, flags, received, own, added, send):
    extra = [] if added is None else [added]

    def body(flags_ref, received_ref, own_ref, *rest):
        added_ref = rest[0] if extra else None
        send_ref, next_ref, *moment_refs = rest[len(extra) :]
        first = flags_ref[1] == 0
        for slot, cols in plan.halves(flags_ref):
            for f in range(3):
                value = jnp.where(first, own_ref[f, :, cols], received_ref[f, :, cols])
                next_ref[f, :, cols] = value if added_ref is None else value + added_ref[f, :, cols]
            plan.emit_moments(slot, cols, next_ref, send_ref, moment_refs)

    operands = [flags, received, own, *extra, send]
    return on_chip_call(body, operands, [plan.state, *plan.moments], name="select_state")


def stage_call(plan, flags, stage, state, grad_x, received, turning, apply, send, others):
    mine, other, mate = received
    count = len(mine)
    with_moments = stage in (1, 2)

    def body(flags_ref, state_ref, grad_ref, turning_ref, *rest):
        pair_refs, rest = (rest[:count], rest[count : 2 * count]), rest[2 * count :]
        mate_ref, apply_ref, rest = rest[0], rest[1], rest[2:]
        other_ins, rest = rest[: len(others)], rest[len(others) :]
        if with_moments:
            send_ref, rest = rest[0], rest[1:]
        grad_y = rest[-1]
        for slot, cols in plan.halves(flags_ref):
            for f in range(3):
                grad_y[f] = plan.y_gradient(f, cols, state_ref, pair_refs[slot], mate_ref, apply_ref)
            for start in range(0, plan.rows, ROWS):
                at = slice(start, start + ROWS)
                now = [state_ref[f, at, cols] for f in range(3)]
                rates = tendency_rows(
                    *now,
                    [grad_ref[f, at, cols] for f in range(3)],
                    [grad_y[f, at, :] for f in range(3)],
                    turning_ref[at, :],
                )
                for f in range(3):
                    ahead = now[f] + HALF_STEP * rates[f]
                    if stage in (1, 2):
                        rest[0][f, at, cols] = ahead
                        rest[1][f, at, cols] = rates[f]
                    elif stage == 3:
                        rest[0][f, at, cols] = ahead
                        olds = (other_ins[0][f, at, cols], other_ins[1][f, at, cols], rates[f])
                        for out, weights in ((rest[1], CORRECT_FIRST), (rest[2], CORRECT_SECOND)):
                            out[f, at, cols] = sum((STEP_LENGTH * w) * r for w, r in zip(weights, olds))
                    else:
                        rest[0][f, at, cols] = ahead + other_ins[0][f, at, cols]
            if with_moments:
                plan.emit_moments(slot, cols, rest[0], send_ref, rest[2:5])

    operands = [flags, state, grad_x, turning, *mine, *other, mate, apply, *others]
    if with_moments:
        operands.append(send)
    state_outs = {1: 2, 2: 2, 3: 3, 4: 1}[stage]
    shapes = [plan.state] * state_outs + (list(plan.moments) if with_moments else [])
    return on_chip_call(
        body,
        operands,
        shapes,
        keep=stage != 4,
        scratch_shapes=[pltpu.VMEM((3, plan.rows, plan.half), F32)],
        name=f"stage_{stage}",
    )


def ahead_in_time(array):
    size = lax.axis_size("tm")
    return lax.ppermute(array, "tm", [(i, i + 1) for i in range(size - 1)])


def mate_swap(array):
    size = lax.axis_size("grid")
    return lax.ppermute(array, "grid", [(i, i ^ 1) for i in range(size)])


def exchange(plan, mine, theirs, to_mate):
    size = lax.axis_size("grid")
    from_mate = mate_swap(to_mate)
    merged = mine + mate_swap(theirs)
    mine_in, other_in, start = [], [], 0
    for d, rank in enumerate(plan.ranks, 1):
        part = merged[:, start : start + rank]
        start += rank
        mine_in.append(lax.ppermute(part, "grid", [(i, (i + 2 * d) % size) for i in range(size)]))
    for part in mine_in:
        other_in.append(mate_swap(part))
    return mine_in, other_in, from_mate


def per_device(starts, coriolis):
    first_state = starts[0]
    _, rows, length = first_state.shape
    ranks, mate_rank, send_tables, apply_tables = y_tables(length, lax.axis_size("grid"))
    plan = Plan(rows, length, ranks, mate_rank)
    member = lax.axis_index("grid") % 2
    flags = jnp.stack([member, lax.axis_index("tm")]).astype(jnp.int32)
    table = jnp.asarray(x_tables(length))
    send = lax.dynamic_index_in_dim(jnp.asarray(send_tables), member, 0, keepdims=False)
    apply = lax.dynamic_index_in_dim(jnp.asarray(apply_tables), member, 0, keepdims=False)
    turning = coriolis[:, None]

    def stage(number, state, moments, others=()):
        received = exchange(plan, *moments)
        grad_x = along_x(state, table)
        return stage_call(plan, flags, number, state, grad_x, received, turning, apply, send, others)

    before = ahead_in_time(first_state)
    node_zero, *moments = select_call(plan, flags, before, first_state, None, send)
    node_one, rate_zero, *moments = stage(1, node_zero, moments)
    node_two, rate_one, *moments = stage(2, node_one, moments)
    lead, add_first, add_second = stage(3, node_two, moments, (rate_zero, rate_one))
    came = ahead_in_time(lead)
    node, *moments = select_call(plan, flags, came, node_one, add_first, send)
    (ends,) = stage(4, node, moments, (add_second,))
    return ends[None]


def solution(mesh):
    return jax.shard_map(
        per_device,
        mesh=mesh,
        in_specs=(P("tm", None, "grid", None), P("grid")),
        out_specs=P("tm", None, "grid", None),
        check_vma=False,
    )
```

```python
import functools
import math

import jax
import jax.numpy as jnp
import ml_dtypes
import numpy as np
from jax import lax
from jax.experimental import pallas as pl
from jax.experimental.pallas import tpu as pltpu
from jax.sharding import PartitionSpec as P

SWEEPS = 2
STEP_LENGTH = 0.001
HALF_STEP = 0.5 * STEP_LENGTH
GRAVITY = 1.0
CORRECT_FIRST = (5.0 / 24.0 - 0.5, 8.0 / 24.0, -1.0 / 24.0)
CORRECT_SECOND = (-1.0 / 24.0, 8.0 / 24.0 - 0.5, 5.0 / 24.0)
TOLERANCE = 1e-8
ROWS = 8
KERNEL_BYTES = 8 * 2**20
KERNEL_FLOPS = 10**10
F32 = jnp.float32
BF16 = jnp.bfloat16


def kernel_values(length):
    values = np.zeros(length)
    for j in range(1, length):
        values[j] = (0.5 if j % 2 == 0 else -0.5) / math.tan(math.pi * j / length)
    values[length // 2] = 0.0
    return values


def toeplitz(values, rows, cols, offset):
    index = np.arange(rows)[:, None] - np.arange(cols)[None, :] + offset
    return values[index % len(values)]


def cross_factors(block, tolerance):
    rest = block.copy()
    lefts, rights = [], []
    while True:
        at = int(np.argmax(np.abs(rest)))
        i, j = divmod(at, rest.shape[1])
        pivot = rest[i, j]
        small = abs(pivot) <= tolerance
        if (small and lefts and len(lefts) % 8 == 0) or len(lefts) == block.shape[0]:
            break
        if abs(pivot) == 0.0:
            left, right = np.zeros(rest.shape[0]), np.zeros(rest.shape[1])
        else:
            left, right = rest[:, j] / pivot, rest[i, :].copy()
        lefts.append(left)
        rights.append(right)
        rest = rest - left[:, None] * right[None, :]
    return np.stack(lefts, axis=1), np.stack(rights, axis=0)


def two_parts(table):
    high = table.astype(ml_dtypes.bfloat16)
    low = (table - high.astype(np.float64)).astype(ml_dtypes.bfloat16)
    return high, low


def pad_rows(table, multiple):
    extra = -table.shape[0] % multiple
    return np.pad(table, ((0, extra), (0, 0)))


def x_tables(length):
    values = kernel_values(length)
    half = length // 2
    near = toeplitz(values, half, half, 0).T
    far = toeplitz(values, half, half, half).T
    plus = two_parts(0.5 * (near + far))
    minus = two_parts(0.5 * (near - far))
    return np.stack([plus[0], plus[1], minus[0], minus[1]])


@functools.lru_cache(maxsize=None)
def y_tables(length, devices):
    rows = length // devices
    pair = 2 * rows
    pairs = devices // 2
    values = kernel_values(length)
    tolerance = TOLERANCE * float(np.max(np.abs(values)))
    factors = [cross_factors(toeplitz(values, pair, pair, d * pair), tolerance) for d in range(1, pairs)]
    ranks = tuple(f[0].shape[1] for f in factors)
    mates = [cross_factors(toeplitz(values, rows, rows, rows if k == 0 else -rows), tolerance) for k in range(2)]
    mate_rank = max(m[0].shape[1] for m in mates)
    send, apply = [], []
    for k in range(2):
        span = slice(k * rows, (k + 1) * rows)
        to_mate = np.pad(mates[k][1], ((0, mate_rank - mates[k][1].shape[0]), (0, 0)))
        from_mate = np.pad(mates[1 - k][0], ((0, 0), (0, mate_rank - mates[1 - k][0].shape[1])))
        down = pad_rows(np.concatenate([f[1][:, span] for f in factors] + [to_mate], axis=0), 16)
        send.append(np.concatenate(two_parts(down), axis=0))
        own = pad_rows(toeplitz(values, rows, rows, 0).T, 16).T
        up = np.concatenate([own] + [f[0][span] for f in factors] + [from_mate], axis=1)
        up = pad_rows(up.T, 16).T
        apply.append(np.concatenate(two_parts(up), axis=0))
    return ranks, mate_rank, np.stack(send), np.stack(apply)


COST = pl.CostEstimate(flops=KERNEL_FLOPS, transcendentals=0, bytes_accessed=2**20)


def parts_of(value):
    high = value.astype(BF16)
    return high, (value - high.astype(F32)).astype(BF16)


def dot(left, right):
    return jnp.dot(left, right, preferred_element_type=F32)


def product(stacked, high, low):
    count = stacked.shape[0] // 2
    both = dot(stacked, high)
    return both[:count] + both[count:] + dot(stacked[:count], low)


VMEM = pl.BlockSpec(memory_space=pltpu.VMEM)
SMEM = pl.BlockSpec(memory_space=pltpu.SMEM)
ANY = pl.BlockSpec(memory_space=pl.ANY)


def on_chip_call(body, operands, shapes, scalars=1, keep=True, **options):
    held = [pltpu.with_memory_space_constraint(a, pltpu.VMEM) for a in operands[scalars:]]
    outs = [pltpu.VMEM(s.shape, s.dtype) for s in shapes] if keep else shapes
    return pl.pallas_call(
        body,
        in_specs=[SMEM] * scalars + [VMEM] * len(held),
        out_specs=[VMEM] * len(outs),
        out_shape=outs,
        compiler_params=pltpu.CompilerParams(vmem_limit_bytes=KERNEL_BYTES),
        cost_estimate=COST,
        **options,
    )(*operands[:scalars], *held)


def x_kernel(theirs_ref, mine_ref, table_ref, grad_theirs_ref, grad_mine_ref):
    theirs, mine = theirs_ref[...], mine_ref[...]

    def folded(total, at):
        high, low = parts_of(total)
        return dot(high, table_ref[at]) + dot(low, table_ref[at]) + dot(high, table_ref[at + 1])

    even = folded(mine + theirs, 0)
    odd = folded(mine - theirs, 2)
    grad_mine_ref[...] = even + odd
    grad_theirs_ref[...] = even - odd


def along_x(theirs, mine, table):
    fields, rows, half = mine.shape
    flat = [a.reshape(fields * rows, half) for a in (theirs, mine)]
    shape = jax.ShapeDtypeStruct(flat[0].shape, F32)
    grads = on_chip_call(x_kernel, [*flat, table], [shape, shape], scalars=0, name="along_x")
    return [g.reshape(mine.shape) for g in grads]


class Plan:
    def __init__(self, rows, length, ranks, mate_rank):
        self.rows, self.length, self.half = rows, length, length // 2
        self.ranks, self.mate_rank, self.total = ranks, mate_rank, sum(ranks)
        self.state = jax.ShapeDtypeStruct((3, rows, self.half), F32)
        self.whole = jax.ShapeDtypeStruct((3, rows, length), F32)
        self.moments = [jax.ShapeDtypeStruct((3, self.total + mate_rank, self.half), F32)]

    def columns(self, flags_ref, mine):
        member = flags_ref[0]
        at = member if mine else 1 - member
        return pl.ds(pl.multiple_of(at * self.half, 128), self.half)

    def emit_moments(self, next_ref, send_ref, moments_ref):
        for f in range(3):
            found = product(send_ref[...], *parts_of(next_ref[f]))
            moments_ref[f] = found[: self.total + self.mate_rank]

    def y_gradient(self, f, state_ref, pair_refs, mate_ref, apply_ref):
        pieces = [state_ref[f]]
        if self.rows % 16:
            pieces.append(jnp.zeros((-self.rows % 16, self.half), F32))
        pieces += [ref[f] for ref in pair_refs]
        pieces.append(mate_ref[f, mate_ref.shape[1] - self.mate_rank :])
        width = apply_ref.shape[1] - sum(p.shape[0] for p in pieces)
        if width:
            pieces.append(jnp.zeros((width, self.half), F32))
        return product(apply_ref[...], *parts_of(jnp.concatenate(pieces, axis=0)))


def tendency_rows(h, u, v, gx, gy, turning):
    rate_h = -(u * gx[0] + v * gy[0]) - (1.0 + h) * (gx[1] + gy[2])
    rate_u = -(u * gx[1] + v * gy[1]) + turning * v - GRAVITY * gx[0]
    rate_v = -(u * gx[2] + v * gy[2]) - turning * u - GRAVITY * gy[0]
    return rate_h, rate_u, rate_v


def enter_call(plan, flags, state, received, send):
    sources = [state, *received]

    def body(flags_ref, own_ref, *refs):
        received_refs, (send_ref, *outs) = refs[: len(received)], refs[len(received) :]
        nexts, moments, arrived = outs[0:4:2], outs[1:4:2], outs[-1]

        def copy(source_ref, at):
            cols = plan.columns(flags_ref, at == 1)
            return pltpu.make_async_copy(source_ref.at[:, :, cols], nexts[at], arrived.at[at])

        def start(source_ref):
            for at in range(2):
                copy(source_ref, at).start()

        if received:
            pl.when(flags_ref[1] == 0)(lambda: start(own_ref))
            pl.when(flags_ref[1] != 0)(lambda: start(received_refs[0]))
        else:
            start(own_ref)
        for at in range(2):
            copy(own_ref, at).wait()
            plan.emit_moments(nexts[at], send_ref, moments[at])

    shapes = [plan.state, *plan.moments] * 2
    return pl.pallas_call(
        body,
        in_specs=[SMEM] + [ANY] * len(sources) + [VMEM],
        out_specs=[VMEM] * 4,
        out_shape=[pltpu.VMEM(s.shape, s.dtype) for s in shapes],
        scratch_shapes=[pltpu.SemaphoreType.DMA((2,))],
        compiler_params=pltpu.CompilerParams(vmem_limit_bytes=KERNEL_BYTES),
        cost_estimate=COST,
        name="enter",
    )(flags, *sources, pltpu.with_memory_space_constraint(send, pltpu.VMEM))


def restart_call(plan, flags, received, second, node_one, added, send):
    extra = list(second)
    fields = len(received)

    def body(flags_ref, *refs):
        received_refs, (node_ref, added_ref, *rest) = refs[:fields], refs[fields:]
        send_ref, next_ref, moments_ref = rest[len(extra) :]
        for f in range(3):
            value = received_refs[f][...]
            if extra:
                value = jnp.where(flags_ref[1] == 1, rest[f][...], value)
            next_ref[f] = jnp.where(flags_ref[1] == 0, node_ref[f], value) + added_ref[f]
        plan.emit_moments(next_ref, send_ref, moments_ref)

    operands = [flags, *received, node_one, added, *extra, send]
    return on_chip_call(body, operands, [plan.state, *plan.moments], name="restart")


def stage_call(plan, kind, state, grad_x, pair_in, mate_in, turning, apply, send=None, others=()):
    count = len(pair_in)
    split = kind in ("lead", "correct")

    def body(state_ref, grad_ref, turning_ref, *rest):
        pair_refs, (mate_ref, apply_ref), rest = rest[:count], rest[count : count + 2], rest[count + 2 :]
        other_refs, rest = rest[: len(others)], rest[len(others) :]
        if send is not None:
            send_ref, rest = rest[0], rest[1:]
        grad_y = rest[-1]
        for f in range(3):
            grad_y[f] = plan.y_gradient(f, state_ref, pair_refs, mate_ref, apply_ref)
        for start in range(0, plan.rows, ROWS):
            at = slice(start, start + ROWS)
            now = [state_ref[f, at] for f in range(3)]
            rates = tendency_rows(
                *now, [grad_ref[f, at] for f in range(3)], [grad_y[f, at] for f in range(3)], turning_ref[at]
            )
            for f in range(3):
                ahead = now[f] + HALF_STEP * rates[f]
                if kind == "end":
                    ahead = ahead + other_refs[0][f, at]
                if split:
                    rest[f][at] = ahead
                else:
                    rest[0][f, at] = ahead
                if kind == "keep":
                    rest[1][f, at] = rates[f]
                if kind == "correct":
                    olds = (other_refs[0][f, at], other_refs[1][f, at], rates[f])
                    for out, weights in ((rest[-3], CORRECT_FIRST), (rest[-2], CORRECT_SECOND)):
                        out[f, at] = sum((STEP_LENGTH * w) * r for w, r in zip(weights, olds))
        if send is not None:
            plan.emit_moments(rest[0], send_ref, rest[-2])

    operands = [state, grad_x, turning, *pair_in, mate_in, apply, *others]
    shapes = [plan.state] * {"move": 1, "keep": 2, "lead": 0, "correct": 2, "end": 1}[kind]
    if split:
        shapes = [jax.ShapeDtypeStruct(plan.state.shape[1:], F32)] * 3 + shapes
    if send is not None:
        operands.append(send)
        shapes += plan.moments
    return on_chip_call(
        body,
        operands,
        shapes,
        scalars=0,
        scratch_shapes=[pltpu.VMEM((3, plan.rows, plan.half), F32)],
        name=f"stage_{kind}",
    )


def join_call(plan, flags, theirs, mine):
    def body(flags_ref, theirs_ref, mine_ref, out_ref, done):
        copies = [
            pltpu.make_async_copy(ref, out_ref.at[:, :, plan.columns(flags_ref, at == 1)], done.at[at])
            for at, ref in enumerate((theirs_ref, mine_ref))
        ]
        for copy in copies:
            copy.start()
        for copy in copies:
            copy.wait()

    held = [pltpu.with_memory_space_constraint(a, pltpu.VMEM) for a in (theirs, mine)]
    return pl.pallas_call(
        body,
        in_specs=[SMEM, VMEM, VMEM],
        out_specs=ANY,
        out_shape=plan.whole,
        scratch_shapes=[pltpu.SemaphoreType.DMA((2,))],
        compiler_params=pltpu.CompilerParams(vmem_limit_bytes=KERNEL_BYTES),
        name="join",
    )(flags, *held)


def ahead_in_time(array, by):
    size = lax.axis_size("tm")
    return lax.ppermute(array, "tm", [(i, i + by) for i in range(size - by)])


def mate_swap(array):
    size = lax.axis_size("grid")
    return lax.ppermute(array, "grid", [(i, i ^ 1) for i in range(size)])


def exchange(plan, theirs, mine):
    size = lax.axis_size("grid")
    from_mate = mate_swap(theirs)
    mate_first = mate_swap(mine[:, plan.total :])
    merged = mine[:, : plan.total] + from_mate[:, : plan.total]
    first, start = [], 0
    for d, rank in enumerate(plan.ranks, 1):
        part = merged[:, start : start + rank]
        start += rank
        first.append(lax.ppermute(part, "grid", [(i, ((i + 2 * d) % size) ^ 1) for i in range(size)]))
    return (first, mate_first), ([mate_swap(part) for part in first], from_mate)


def per_device(starts, coriolis):
    own = starts[0]
    _, rows, length = own.shape
    ranks, mate_rank, send_tables, apply_tables = y_tables(length, lax.axis_size("grid"))
    plan = Plan(rows, length, ranks, mate_rank)
    member = lax.axis_index("grid") % 2
    flags = jnp.stack([member, lax.axis_index("tm")]).astype(jnp.int32)
    table = jnp.asarray(x_tables(length))
    send = lax.dynamic_index_in_dim(jnp.asarray(send_tables), member, 0, keepdims=False)
    apply = lax.dynamic_index_in_dim(jnp.asarray(apply_tables), member, 0, keepdims=False)
    turning = coriolis[:, None]

    def stage(kind, states, moments, others=((), ()), sends=True, only_first=False):
        received = exchange(plan, *moments)
        grads = along_x(*states, table)
        results = []
        for at in range(1 if only_first else 2):
            pair_in, mate_in = received[at]
            results.append(
                stage_call(
                    plan, kind, states[at], grads[at], pair_in, mate_in, turning, apply, send if sends else None, others[at]
                )
            )
        if not sends:
            return results
        return *zip(*[r[:-1] for r in results]), [r[-1] for r in results]

    def enter(received):
        theirs, theirs_moments, mine, mine_moments = enter_call(plan, flags, own, received, send)
        return [theirs, mine], [theirs_moments, mine_moments]

    before = [ahead_in_time(own, 1)]
    states, moments = enter([])
    states, moments = stage("move", states, moments)
    states, moments = stage("move", states, moments)
    (lead,) = stage("lead", states, moments, sends=False, only_first=True)
    far = [ahead_in_time(field, 2) for field in lead]

    *before, _ = lax.optimization_barrier((*before, lead[0]))
    states, moments = enter(before)
    nodes_one, rates_zero, moments = stage("keep", states, moments)
    states, rates_one, moments = stage("keep", nodes_one, moments)
    moments[0], far[0] = lax.optimization_barrier((moments[0], far[0]))
    theirs, mine = stage("correct", states, moments, list(zip(rates_zero, rates_one)), sends=False)
    near = [ahead_in_time(field, 1) for field in mine[:3]]

    results = [
        restart_call(plan, flags, far, theirs[:3], nodes_one[0], theirs[3], send),
        restart_call(plan, flags, near, (), nodes_one[1], mine[3], send),
    ]
    ends = stage("end", [r[0] for r in results], [r[1] for r in results], ((theirs[4],), (mine[4],)), sends=False)
    return join_call(plan, flags, ends[0][0], ends[1][0])[None]


def solution(mesh):
    return jax.shard_map(
        per_device,
        mesh=mesh,
        in_specs=(P("tm", None, "grid", None), P("grid")),
        out_specs=P("tm", None, "grid", None),
        check_vma=False,
    )
```

```python
import functools
import math

import jax
import jax.numpy as jnp
import ml_dtypes
import numpy as np
from jax import lax
from jax.experimental import pallas as pl
from jax.experimental.pallas import tpu as pltpu
from jax.sharding import PartitionSpec as P

SWEEPS = 2
STEP_LENGTH = 0.001
HALF_STEP = 0.5 * STEP_LENGTH
GRAVITY = 1.0
CORRECT_FIRST = (5.0 / 24.0 - 0.5, 8.0 / 24.0, -1.0 / 24.0)
CORRECT_SECOND = (-1.0 / 24.0, 8.0 / 24.0 - 0.5, 5.0 / 24.0)
TOLERANCE = 1e-8
ROWS = 8
KERNEL_BYTES = 8 * 2**20
KERNEL_FLOPS = 10**10
FAR = (3,)
NEAR = (3,)
F32 = jnp.float32
BF16 = jnp.bfloat16


def kernel_values(length):
    values = np.zeros(length)
    for j in range(1, length):
        values[j] = (0.5 if j % 2 == 0 else -0.5) / math.tan(math.pi * j / length)
    values[length // 2] = 0.0
    return values


def toeplitz(values, rows, cols, offset):
    index = np.arange(rows)[:, None] - np.arange(cols)[None, :] + offset
    return values[index % len(values)]


def cross_factors(block, tolerance):
    rest = block.copy()
    lefts, rights = [], []
    while True:
        at = int(np.argmax(np.abs(rest)))
        i, j = divmod(at, rest.shape[1])
        pivot = rest[i, j]
        small = abs(pivot) <= tolerance
        if (small and lefts and len(lefts) % 8 == 0) or len(lefts) == block.shape[0]:
            break
        if abs(pivot) == 0.0:
            left, right = np.zeros(rest.shape[0]), np.zeros(rest.shape[1])
        else:
            left, right = rest[:, j] / pivot, rest[i, :].copy()
        lefts.append(left)
        rights.append(right)
        rest = rest - left[:, None] * right[None, :]
    return np.stack(lefts, axis=1), np.stack(rights, axis=0)


def two_parts(table):
    high = table.astype(ml_dtypes.bfloat16)
    low = (table - high.astype(np.float64)).astype(ml_dtypes.bfloat16)
    return high, low


def pad_rows(table, multiple):
    extra = -table.shape[0] % multiple
    return np.pad(table, ((0, extra), (0, 0)))


def x_tables(length):
    values = kernel_values(length)
    half = length // 2
    near = toeplitz(values, half, half, 0).T
    far = toeplitz(values, half, half, half).T
    plus = two_parts(0.5 * (near + far))
    minus = two_parts(0.5 * (near - far))
    return np.stack([plus[0], plus[1], minus[0], minus[1]])


@functools.lru_cache(maxsize=None)
def y_tables(length, devices):
    rows = length // devices
    pair = 2 * rows
    pairs = devices // 2
    values = kernel_values(length)
    tolerance = TOLERANCE * float(np.max(np.abs(values)))
    factors = [cross_factors(toeplitz(values, pair, pair, d * pair), tolerance) for d in range(1, pairs)]
    ranks = tuple(f[0].shape[1] for f in factors)
    mates = [cross_factors(toeplitz(values, rows, rows, rows if k == 0 else -rows), tolerance) for k in range(2)]
    mate_rank = max(m[0].shape[1] for m in mates)
    send, apply = [], []
    for k in range(2):
        span = slice(k * rows, (k + 1) * rows)
        to_mate = np.pad(mates[k][1], ((0, mate_rank - mates[k][1].shape[0]), (0, 0)))
        from_mate = np.pad(mates[1 - k][0], ((0, 0), (0, mate_rank - mates[1 - k][0].shape[1])))
        down = pad_rows(np.concatenate([f[1][:, span] for f in factors] + [to_mate], axis=0), 16)
        send.append(np.concatenate(two_parts(down), axis=0))
        own = pad_rows(toeplitz(values, rows, rows, 0).T, 16).T
        up = np.concatenate([own] + [f[0][span] for f in factors] + [from_mate], axis=1)
        up = pad_rows(up.T, 16).T
        apply.append(np.concatenate(two_parts(up), axis=0))
    return ranks, mate_rank, np.stack(send), np.stack(apply)


COST = pl.CostEstimate(flops=KERNEL_FLOPS, transcendentals=0, bytes_accessed=2**20)


def parts_of(value):
    high = value.astype(BF16)
    return high, (value - high.astype(F32)).astype(BF16)


def dot(left, right):
    return jnp.dot(left, right, preferred_element_type=F32)


def product(stacked, high, low):
    count = stacked.shape[0] // 2
    both = dot(stacked, high)
    return both[:count] + both[count:] + dot(stacked[:count], low)


VMEM = pl.BlockSpec(memory_space=pltpu.VMEM)
HBM = pl.BlockSpec(memory_space=pltpu.HBM)


def on_chip_call(body, operands, shapes, keep=True, **options):
    held = [pltpu.with_memory_space_constraint(a, pltpu.VMEM) for a in operands]
    outs = [pltpu.VMEM(s.shape, s.dtype) for s in shapes] if keep else shapes
    return pl.pallas_call(
        body,
        in_specs=[VMEM] * len(held),
        out_specs=[VMEM if keep else HBM] * len(outs),
        out_shape=outs,
        compiler_params=pltpu.CompilerParams(vmem_limit_bytes=KERNEL_BYTES),
        cost_estimate=COST,
        **options,
    )(*held)


def x_kernel(theirs_ref, mine_ref, table_ref, grad_theirs_ref, grad_mine_ref):
    theirs, mine = theirs_ref[...], mine_ref[...]

    def folded(total, at):
        high, low = parts_of(total)
        return dot(high, table_ref[at]) + dot(low, table_ref[at]) + dot(high, table_ref[at + 1])

    even = folded(mine + theirs, 0)
    odd = folded(mine - theirs, 2)
    grad_mine_ref[...] = even + odd
    grad_theirs_ref[...] = even - odd


def along_x(theirs, mine, table):
    fields, rows, half = mine.shape
    flat = [a.reshape(fields * rows, half) for a in (theirs, mine)]
    shape = jax.ShapeDtypeStruct(flat[0].shape, F32)
    grads = on_chip_call(x_kernel, [*flat, table], [shape, shape], name="along_x")
    return [g.reshape(mine.shape) for g in grads]


def member_of_pair():
    return lax.rem(lax.axis_index("grid"), 2)


class Plan:
    def __init__(self, rows, length, ranks, mate_rank):
        self.rows, self.length, self.half = rows, length, length // 2
        self.ranks, self.mate_rank, self.total = ranks, mate_rank, sum(ranks)
        self.state = jax.ShapeDtypeStruct((3, rows, self.half), F32)
        self.whole = jax.ShapeDtypeStruct((3, rows, length), F32)
        self.moments = [jax.ShapeDtypeStruct((3, self.total + mate_rank, self.half), F32)]

    def columns(self, mine):
        at = member_of_pair() if mine else 1 - member_of_pair()
        return pl.ds(pl.multiple_of(at * self.half, 128), self.half)

    def emit_moments(self, next_ref, send_ref, moments_ref):
        for f in range(3):
            found = product(send_ref[...], *parts_of(next_ref[f]))
            moments_ref[f] = found[: self.total + self.mate_rank]

    def y_gradient(self, f, state_ref, pair_refs, mate_ref, apply_ref):
        pieces = [state_ref[f]]
        if self.rows % 16:
            pieces.append(jnp.zeros((-self.rows % 16, self.half), F32))
        pieces += [ref[f] for ref in pair_refs]
        pieces.append(mate_ref[f, mate_ref.shape[1] - self.mate_rank :])
        width = apply_ref.shape[1] - sum(p.shape[0] for p in pieces)
        if width:
            pieces.append(jnp.zeros((width, self.half), F32))
        return product(apply_ref[...], *parts_of(jnp.concatenate(pieces, axis=0)))


def tendency_rows(h, u, v, gx, gy, turning):
    rate_h = -(u * gx[0] + v * gy[0]) - (1.0 + h) * (gx[1] + gy[2])
    rate_u = -(u * gx[1] + v * gy[1]) + turning * v - GRAVITY * gx[0]
    rate_v = -(u * gx[2] + v * gy[2]) - turning * u - GRAVITY * gy[0]
    return rate_h, rate_u, rate_v


def enter_call(plan, state, received, send, coriolis=None, both_apply=None):
    sources = [state, *received]
    opening = coriolis is not None
    more = [both_apply, coriolis] if opening else []

    def body(own_ref, *refs):
        received_refs, (send_ref, *refs) = refs[: len(received)], refs[len(received) :]
        more_refs, outs = refs[: len(more)], refs[len(more) :]
        nexts, moments, arrived = outs[0:4:2], outs[1:4:2], outs[-1]

        def copy(source_ref, at):
            cols = plan.columns(at == 1)
            return pltpu.make_async_copy(source_ref.at[:, :, cols], nexts[at], arrived.at[at])

        def start(source_ref):
            for at in range(2):
                copy(source_ref, at).start()

        if received:
            pl.when(lax.axis_index("tm") == 0)(lambda: start(own_ref))
            pl.when(lax.axis_index("tm") != 0)(lambda: start(received_refs[0]))
        else:
            start(own_ref)
        if opening:
            outs[4][...] = send_ref[member_of_pair()]
            outs[5][...] = more_refs[0][member_of_pair()]
            square = (plan.rows, plan.rows)
            here = lax.broadcasted_iota(jnp.int32, square, 0) == lax.broadcasted_iota(jnp.int32, square, 1)
            outs[6][...] = jnp.sum(jnp.where(here, more_refs[1][...], 0.0), axis=1, keepdims=True)
            send_ref = outs[4]
        for at in range(2):
            copy(own_ref, at).wait()
            plan.emit_moments(nexts[at], send_ref, moments[at])

    shapes = [plan.state, *plan.moments] * 2
    if opening:
        shapes += [jax.ShapeDtypeStruct(a.shape[1:], a.dtype) for a in (send, both_apply)]
        shapes.append(jax.ShapeDtypeStruct((plan.rows, 1), F32))
    return pl.pallas_call(
        body,
        in_specs=[HBM] * len(sources) + [VMEM] * (1 + len(more)),
        out_specs=[VMEM] * len(shapes),
        out_shape=[pltpu.VMEM(s.shape, s.dtype) for s in shapes],
        scratch_shapes=[pltpu.SemaphoreType.DMA((2,))],
        compiler_params=pltpu.CompilerParams(vmem_limit_bytes=KERNEL_BYTES),
        cost_estimate=COST,
        name="enter",
    )(*sources, *[pltpu.with_memory_space_constraint(a, pltpu.VMEM) for a in (send, *more)])


def field_of(refs, f):
    for ref in refs:
        if f < ref.shape[0]:
            return ref[f]
        f -= ref.shape[0]


def restart_call(plan, received, second, node_one, added, send):
    count = len(received)

    def body(*refs):
        received_refs, (node_ref, added_ref, *rest) = refs[:count], refs[count:]
        second_refs, (send_ref, next_ref, moments_ref) = rest[: len(second)], rest[len(second) :]
        for f in range(3):
            value = field_of(received_refs, f)
            if second:
                value = jnp.where(lax.axis_index("tm") == 1, field_of(second_refs, f), value)
            next_ref[f] = jnp.where(lax.axis_index("tm") == 0, node_ref[f], value) + added_ref[f]
        plan.emit_moments(next_ref, send_ref, moments_ref)

    operands = [*received, node_one, added, *second, send]
    return on_chip_call(body, operands, [plan.state, *plan.moments], name="restart")


def stage_call(plan, kind, state, grad_x, pair_in, mate_in, turning, apply, send=None, others=(), groups=()):
    count = len(pair_in)
    join = kind == "join"

    def body(state_ref, grad_ref, turning_ref, *rest):
        pair_refs, (mate_ref, apply_ref), rest = rest[:count], rest[count : count + 2], rest[count + 2 :]
        other_refs, rest = rest[: len(others)], rest[len(others) :]
        if send is not None:
            send_ref, rest = rest[0], rest[1:]
        leads, outs, grad_y = rest[: len(groups)], rest[len(groups) : len(shapes)], rest[len(shapes)]
        if join:
            made_ref, done = rest[len(shapes) + 1 :]
            whole_ref, outs = outs[0], [made_ref]
            copies = [
                pltpu.make_async_copy(ref, whole_ref.at[:, :, plan.columns(at == 1)], done.at[at])
                for at, ref in enumerate((other_refs[1], made_ref))
            ]
            copies[0].start()
        for f in range(3):
            grad_y[f] = plan.y_gradient(f, state_ref, pair_refs, mate_ref, apply_ref)
        for start in range(0, plan.rows, ROWS):
            at = slice(start, start + ROWS)
            now = [state_ref[f, at] for f in range(3)]
            rates = tendency_rows(
                *now, [grad_ref[f, at] for f in range(3)], [grad_y[f, at] for f in range(3)], turning_ref[at]
            )
            for f in range(3):
                ahead = now[f] + HALF_STEP * rates[f]
                if groups:
                    group = next(g for g in range(len(groups)) if f < sum(groups[: g + 1]))
                    leads[group][f - sum(groups[:group]), at] = ahead
                elif kind in ("end", "join"):
                    outs[0][f, at] = ahead + other_refs[0][f, at]
                else:
                    outs[0][f, at] = ahead
                if kind == "keep":
                    outs[1][f, at] = rates[f]
                if kind == "correct":
                    olds = (other_refs[0][f, at], other_refs[1][f, at], rates[f])
                    for out, weights in zip(outs, (CORRECT_FIRST, CORRECT_SECOND)):
                        out[f, at] = sum((STEP_LENGTH * w) * r for w, r in zip(weights, olds))
        if send is not None:
            plan.emit_moments(outs[0], send_ref, outs[-1])
        if join:
            copies[1].start()
            for copy in copies:
                copy.wait()

    operands = [state, grad_x, turning, *pair_in, mate_in, apply, *others]
    shapes = [jax.ShapeDtypeStruct((g, *plan.state.shape[1:]), F32) for g in groups]
    shapes += [plan.state] * {"move": 1, "keep": 2, "lead": 0, "correct": 2, "end": 1, "join": 0}[kind]
    scratch = [pltpu.VMEM(plan.state.shape, F32)]
    if send is not None:
        operands.append(send)
        shapes += plan.moments
    if join:
        shapes = [plan.whole]
        scratch += [pltpu.VMEM(plan.state.shape, F32), pltpu.SemaphoreType.DMA((2,))]
    return on_chip_call(body, operands, shapes, keep=not join, scratch_shapes=scratch, name=f"stage_{kind}")


def ahead_in_time(array, by):
    size = lax.axis_size("tm")
    return lax.ppermute(array, "tm", [(i, i + by) for i in range(size - by)])


def mate_swap(array):
    size = lax.axis_size("grid")
    return lax.ppermute(array, "grid", [(i, i ^ 1) for i in range(size)])


def exchange(plan, theirs, mine):
    size = lax.axis_size("grid")
    from_mate = mate_swap(theirs)
    mate_first = mate_swap(mine[:, plan.total :])
    merged = mine[:, : plan.total] + from_mate[:, : plan.total]
    first, start = [], 0
    for d, rank in enumerate(plan.ranks, 1):
        part = merged[:, start : start + rank]
        start += rank
        first.append(lax.ppermute(part, "grid", [(i, ((i + 2 * d) % size) ^ 1) for i in range(size)]))
    return (first, mate_first), ([mate_swap(part) for part in first], from_mate)


def per_device(starts, coriolis):
    own = starts[0]
    _, rows, length = own.shape
    ranks, mate_rank, send_tables, apply_tables = y_tables(length, lax.axis_size("grid"))
    plan = Plan(rows, length, ranks, mate_rank)
    table = jnp.asarray(x_tables(length))
    def stage(kinds, states, moments, others=((), ()), sends=False, groups=((), ())):
        received = exchange(plan, *moments)
        grads = along_x(*states, table)
        results = []
        for at, kind in enumerate(kinds):
            more = others[at] if kind != "join" else (*others[at], results[0][0])
            operands = (states[at], grads[at], *received[at], turning, apply)
            results.append(stage_call(plan, kind, *operands, send if sends else None, more, groups[at]))
        if not sends:
            return results
        return *zip(*[r[:-1] for r in results]), [r[-1] for r in results]

    before = ahead_in_time(own, 1)
    both_send, both_apply = jnp.asarray(send_tables), jnp.asarray(apply_tables)
    opened = enter_call(plan, own, [], both_send, coriolis[None, :], both_apply)
    states, moments, (send, apply, turning) = opened[0:4:2], list(opened[1:4:2]), opened[4:]
    states, moments = stage(("move", "move"), states, moments, sends=True)
    states, moments = stage(("move", "move"), states, moments, sends=True)
    (lead,) = stage(("lead",), states, moments, groups=(FAR,))
    far = [ahead_in_time(fields, 2) for fields in lead]

    before, _ = lax.optimization_barrier((before, lead[0]))
    entered = enter_call(plan, own, [before], send)
    states, moments = entered[0::2], list(entered[1::2])
    nodes_one, rates_zero, moments = stage(("keep", "keep"), states, moments, sends=True)
    states, rates_one, moments = stage(("keep", "keep"), nodes_one, moments, sends=True)
    olds = list(zip(rates_zero, rates_one))
    theirs, mine = stage(("correct", "correct"), states, moments, olds, groups=((3,), NEAR))
    near = [ahead_in_time(fields, 1) for fields in mine[: len(NEAR)]]

    results = [
        restart_call(plan, far, theirs[:1], nodes_one[0], theirs[1], send),
        restart_call(plan, near, (), nodes_one[1], mine[-2], send),
    ]
    lasts = ((theirs[2],), (mine[-1],))
    ends = stage(("end", "join"), [r[0] for r in results], [r[1] for r in results], lasts)
    return ends[1][0][None]


def solution(mesh):
    return jax.shard_map(
        per_device,
        mesh=mesh,
        in_specs=(P("tm", None, "grid", None), P("grid")),
        out_specs=P("tm", None, "grid", None),
        check_vma=False,
    )
```

```python
import functools
import math

import jax
import jax.numpy as jnp
import ml_dtypes
import numpy as np
from jax import lax
from jax.experimental import pallas as pl
from jax.experimental.pallas import tpu as pltpu
from jax.sharding import PartitionSpec as P

SWEEPS = 2
STEP_LENGTH = 0.001
HALF_STEP = 0.5 * STEP_LENGTH
GRAVITY = 1.0
CORRECT_FIRST = (5.0 / 24.0 - 0.5, 8.0 / 24.0, -1.0 / 24.0)
CORRECT_SECOND = (-1.0 / 24.0, 8.0 / 24.0 - 0.5, 5.0 / 24.0)
TOLERANCE = 1e-8
ROWS = 8
KERNEL_BYTES = 8 * 2**20
KERNEL_FLOPS = 10**10
FAR = (3,)
NEAR = (3,)
F32 = jnp.float32
BF16 = jnp.bfloat16


def kernel_values(length):
    values = np.zeros(length)
    for j in range(1, length):
        values[j] = (0.5 if j % 2 == 0 else -0.5) / math.tan(math.pi * j / length)
    values[length // 2] = 0.0
    return values


def toeplitz(values, rows, cols, offset):
    index = np.arange(rows)[:, None] - np.arange(cols)[None, :] + offset
    return values[index % len(values)]


def cross_factors(block, tolerance):
    rest = block.copy()
    lefts, rights = [], []
    while True:
        at = int(np.argmax(np.abs(rest)))
        i, j = divmod(at, rest.shape[1])
        pivot = rest[i, j]
        small = abs(pivot) <= tolerance
        if (small and lefts and len(lefts) % 8 == 0) or len(lefts) == block.shape[0]:
            break
        if abs(pivot) == 0.0:
            left, right = np.zeros(rest.shape[0]), np.zeros(rest.shape[1])
        else:
            left, right = rest[:, j] / pivot, rest[i, :].copy()
        lefts.append(left)
        rights.append(right)
        rest = rest - left[:, None] * right[None, :]
    return np.stack(lefts, axis=1), np.stack(rights, axis=0)


def two_parts(table):
    high = table.astype(ml_dtypes.bfloat16)
    low = (table - high.astype(np.float64)).astype(ml_dtypes.bfloat16)
    return high, low


def pad_rows(table, multiple):
    extra = -table.shape[0] % multiple
    return np.pad(table, ((0, extra), (0, 0)))


def x_tables(length):
    values = kernel_values(length)
    half = length // 2
    near = toeplitz(values, half, half, 0).T
    far = toeplitz(values, half, half, half).T
    plus = two_parts(0.5 * (near + far))
    minus = two_parts(0.5 * (near - far))
    return np.stack([plus[0], plus[1], minus[0], minus[1]])


@functools.lru_cache(maxsize=None)
def y_tables(length, devices):
    rows = length // devices
    pair = 2 * rows
    pairs = devices // 2
    values = kernel_values(length)
    tolerance = TOLERANCE * float(np.max(np.abs(values)))
    factors = [cross_factors(toeplitz(values, pair, pair, d * pair), tolerance) for d in range(1, pairs)]
    ranks = tuple(f[0].shape[1] for f in factors)
    mates = [cross_factors(toeplitz(values, rows, rows, rows if k == 0 else -rows), tolerance) for k in range(2)]
    mate_rank = max(m[0].shape[1] for m in mates)
    send, apply = [], []
    for k in range(2):
        span = slice(k * rows, (k + 1) * rows)
        to_mate = np.pad(mates[k][1], ((0, mate_rank - mates[k][1].shape[0]), (0, 0)))
        from_mate = np.pad(mates[1 - k][0], ((0, 0), (0, mate_rank - mates[1 - k][0].shape[1])))
        down = pad_rows(np.concatenate([f[1][:, span] for f in factors] + [to_mate], axis=0), 16)
        send.append(np.concatenate(two_parts(down), axis=0))
        own = pad_rows(toeplitz(values, rows, rows, 0).T, 16).T
        up = np.concatenate([own] + [f[0][span] for f in factors] + [from_mate], axis=1)
        up = pad_rows(up.T, 16).T
        apply.append(np.concatenate(two_parts(up), axis=0))
    return ranks, mate_rank, np.stack(send), np.stack(apply)


COST = pl.CostEstimate(flops=KERNEL_FLOPS, transcendentals=0, bytes_accessed=2**20)


def parts_of(value):
    high = value.astype(BF16)
    return high, (value - high.astype(F32)).astype(BF16)


def dot(left, right):
    return jnp.dot(left, right, preferred_element_type=F32)


def product(stacked, high, low):
    count = stacked.shape[0] // 2
    both = dot(stacked, high)
    return both[:count] + both[count:] + dot(stacked[:count], low)


VMEM = pl.BlockSpec(memory_space=pltpu.VMEM)
HBM = pl.BlockSpec(memory_space=pltpu.HBM)


def on_chip_call(body, operands, shapes, keep=True, **options):
    held = [pltpu.with_memory_space_constraint(a, pltpu.VMEM) for a in operands]
    outs = [pltpu.VMEM(s.shape, s.dtype) for s in shapes] if keep else shapes
    return pl.pallas_call(
        body,
        in_specs=[VMEM] * len(held),
        out_specs=[VMEM if keep else HBM] * len(outs),
        out_shape=outs,
        compiler_params=pltpu.CompilerParams(vmem_limit_bytes=KERNEL_BYTES),
        cost_estimate=COST,
        **options,
    )(*held)


def x_kernel(theirs_ref, mine_ref, table_ref, grad_theirs_ref, grad_mine_ref):
    theirs, mine = theirs_ref[...], mine_ref[...]

    def folded(total, at):
        high, low = parts_of(total)
        return dot(high, table_ref[at]) + dot(low, table_ref[at]) + dot(high, table_ref[at + 1])

    even = folded(mine + theirs, 0)
    odd = folded(mine - theirs, 2)
    grad_mine_ref[...] = even + odd
    grad_theirs_ref[...] = even - odd


def along_x(theirs, mine, table):
    fields, rows, half = mine.shape
    flat = [a.reshape(fields * rows, half) for a in (theirs, mine)]
    shape = jax.ShapeDtypeStruct(flat[0].shape, F32)
    grads = on_chip_call(x_kernel, [*flat, table], [shape, shape], name="along_x")
    return [g.reshape(mine.shape) for g in grads]


def member_of_pair():
    return lax.rem(lax.axis_index("grid"), 2)


class Plan:
    def __init__(self, rows, length, ranks, mate_rank):
        self.rows, self.length, self.half = rows, length, length // 2
        self.ranks, self.mate_rank, self.total = ranks, mate_rank, sum(ranks)
        self.state = jax.ShapeDtypeStruct((3, rows, self.half), F32)
        self.whole = jax.ShapeDtypeStruct((3, rows, length), F32)
        self.moments = [jax.ShapeDtypeStruct((3, self.total + mate_rank, self.half), F32)]

    def columns(self, mine):
        at = member_of_pair() if mine else 1 - member_of_pair()
        return pl.ds(pl.multiple_of(at * self.half, 128), self.half)

    def emit_moments(self, next_ref, send_ref, moments_ref):
        for f in range(3):
            found = product(send_ref[...], *parts_of(next_ref[f]))
            moments_ref[f] = found[: self.total + self.mate_rank]

    def y_gradient(self, f, state_ref, pair_refs, mate_ref, apply_ref):
        pieces = [state_ref[f]]
        if self.rows % 16:
            pieces.append(jnp.zeros((-self.rows % 16, self.half), F32))
        pieces += [ref[f] for ref in pair_refs]
        pieces.append(mate_ref[f, mate_ref.shape[1] - self.mate_rank :])
        width = apply_ref.shape[1] - sum(p.shape[0] for p in pieces)
        if width:
            pieces.append(jnp.zeros((width, self.half), F32))
        return product(apply_ref[...], *parts_of(jnp.concatenate(pieces, axis=0)))


def tendency_rows(h, u, v, gx, gy, turning):
    rate_h = -(u * gx[0] + v * gy[0]) - (1.0 + h) * (gx[1] + gy[2])
    rate_u = -(u * gx[1] + v * gy[1]) + turning * v - GRAVITY * gx[0]
    rate_v = -(u * gx[2] + v * gy[2]) - turning * u - GRAVITY * gy[0]
    return rate_h, rate_u, rate_v


def enter_call(plan, state, received=None, tables=None, send=None):
    sources = [state] if received is None else [state, received]
    opening = tables is not None
    held_in = pltpu.HBM if opening else pltpu.VMEM
    more = [pltpu.with_memory_space_constraint(a, held_in) for a in (tables if opening else [send])]

    def body(*refs):
        source_refs, refs = refs[: len(sources)], refs[len(sources) :]
        more_refs, outs = refs[: len(more)], refs[len(more) :]
        nexts, moments, arrived = outs[0:4:2], outs[1:4:2], outs[-1]

        def copy(source_ref, at):
            return pltpu.make_async_copy(source_ref.at[:, :, plan.columns(at == 1)], nexts[at], arrived.at[at])

        def start(source_ref):
            for at in range(2):
                copy(source_ref, at).start()

        if opening:
            picks = [
                pltpu.make_async_copy(more_refs[n].at[member_of_pair()], outs[4 + n], arrived.at[2 + n]) for n in range(2)
            ]
            picks.append(pltpu.make_async_copy(more_refs[2], outs[-2], arrived.at[4]))
            for pick in picks:
                pick.start()
            start(source_refs[0])
            for pick in picks:
                pick.wait()
            square = (plan.rows, plan.rows)
            here = lax.broadcasted_iota(jnp.int32, square, 0) == lax.broadcasted_iota(jnp.int32, square, 1)
            outs[6][...] = jnp.sum(jnp.where(here, outs[-2][...], 0.0), axis=1, keepdims=True)
        else:
            first = lax.axis_index("tm") == 0
            pl.when(first)(lambda: start(source_refs[0]))
            pl.when(jnp.logical_not(first))(lambda: start(source_refs[1]))
        send_ref = outs[4] if opening else more_refs[0]
        for at in range(2):
            copy(source_refs[0], at).wait()
            plan.emit_moments(nexts[at], send_ref, moments[at])

    shapes = [plan.state, *plan.moments] * 2
    scratch = [pltpu.SemaphoreType.DMA((5,))]
    if opening:
        shapes += [jax.ShapeDtypeStruct(a.shape[1:], a.dtype) for a in tables[:2]]
        shapes.append(jax.ShapeDtypeStruct((plan.rows, 1), F32))
        scratch.insert(0, pltpu.VMEM((1, plan.rows), F32))
    return pl.pallas_call(
        body,
        in_specs=[HBM] * len(sources) + [HBM if opening else VMEM] * len(more),
        out_specs=[VMEM] * len(shapes),
        out_shape=[pltpu.VMEM(s.shape, s.dtype) for s in shapes],
        scratch_shapes=scratch,
        compiler_params=pltpu.CompilerParams(vmem_limit_bytes=KERNEL_BYTES),
        cost_estimate=COST,
        name="enter",
    )(*sources, *more)


def field_of(refs, f):
    for ref in refs:
        if f < ref.shape[0]:
            return ref[f]
        f -= ref.shape[0]


def restart_call(plan, received, second, node_one, added, send):
    count = len(received)

    def body(*refs):
        received_refs, (node_ref, added_ref, *rest) = refs[:count], refs[count:]
        second_refs, (send_ref, next_ref, moments_ref) = rest[: len(second)], rest[len(second) :]
        for f in range(3):
            value = field_of(received_refs, f)
            if second:
                value = jnp.where(lax.axis_index("tm") == 1, field_of(second_refs, f), value)
            next_ref[f] = jnp.where(lax.axis_index("tm") == 0, node_ref[f], value) + added_ref[f]
        plan.emit_moments(next_ref, send_ref, moments_ref)

    operands = [*received, node_one, added, *second, send]
    return on_chip_call(body, operands, [plan.state, *plan.moments], name="restart")


def stage_call(plan, kind, state, grad_x, pair_in, mate_in, turning, apply, send=None, others=(), groups=()):
    count = len(pair_in)
    join = kind == "join"

    def body(state_ref, grad_ref, turning_ref, *rest):
        pair_refs, (mate_ref, apply_ref), rest = rest[:count], rest[count : count + 2], rest[count + 2 :]
        other_refs, rest = rest[: len(others)], rest[len(others) :]
        if send is not None:
            send_ref, rest = rest[0], rest[1:]
        leads, outs, grad_y = rest[: len(groups)], rest[len(groups) : len(shapes)], rest[len(shapes)]
        if join:
            made_ref, done = rest[len(shapes) + 1 :]
            whole_ref, outs = outs[0], [made_ref]
            copies = [
                pltpu.make_async_copy(ref, whole_ref.at[:, :, plan.columns(at == 1)], done.at[at])
                for at, ref in enumerate((other_refs[1], made_ref))
            ]
            copies[0].start()
        for f in range(3):
            grad_y[f] = plan.y_gradient(f, state_ref, pair_refs, mate_ref, apply_ref)
        for start in range(0, plan.rows, ROWS):
            at = slice(start, start + ROWS)
            now = [state_ref[f, at] for f in range(3)]
            rates = tendency_rows(
                *now, [grad_ref[f, at] for f in range(3)], [grad_y[f, at] for f in range(3)], turning_ref[at]
            )
            for f in range(3):
                ahead = now[f] + HALF_STEP * rates[f]
                if groups:
                    group = next(g for g in range(len(groups)) if f < sum(groups[: g + 1]))
                    leads[group][f - sum(groups[:group]), at] = ahead
                elif kind in ("end", "join"):
                    outs[0][f, at] = ahead + other_refs[0][f, at]
                else:
                    outs[0][f, at] = ahead
                if kind == "keep":
                    outs[1][f, at] = rates[f]
                if kind == "correct":
                    olds = (other_refs[0][f, at], other_refs[1][f, at], rates[f])
                    for out, weights in zip(outs, (CORRECT_FIRST, CORRECT_SECOND)):
                        out[f, at] = sum((STEP_LENGTH * w) * r for w, r in zip(weights, olds))
        if send is not None:
            plan.emit_moments(outs[0], send_ref, outs[-1])
        if join:
            copies[1].start()
            for copy in copies:
                copy.wait()

    operands = [state, grad_x, turning, *pair_in, mate_in, apply, *others]
    shapes = [jax.ShapeDtypeStruct((g, *plan.state.shape[1:]), F32) for g in groups]
    shapes += [plan.state] * {"move": 1, "keep": 2, "lead": 0, "correct": 2, "end": 1, "join": 0}[kind]
    scratch = [pltpu.VMEM(plan.state.shape, F32)]
    if send is not None:
        operands.append(send)
        shapes += plan.moments
    if join:
        shapes = [plan.whole]
        scratch += [pltpu.VMEM(plan.state.shape, F32), pltpu.SemaphoreType.DMA((2,))]
    return on_chip_call(body, operands, shapes, keep=not join, scratch_shapes=scratch, name=f"stage_{kind}")


def ahead_in_time(array, by):
    size = lax.axis_size("tm")
    return lax.ppermute(array, "tm", [(i, i + by) for i in range(size - by)])


def mate_swap(array):
    size = lax.axis_size("grid")
    return lax.ppermute(array, "grid", [(i, i ^ 1) for i in range(size)])


def exchange(plan, theirs, mine):
    size = lax.axis_size("grid")
    from_mate = mate_swap(theirs)
    mate_first = mate_swap(mine[:, plan.total :])
    merged = mine[:, : plan.total] + from_mate[:, : plan.total]
    first, start = [], 0
    for d, rank in enumerate(plan.ranks, 1):
        part = merged[:, start : start + rank]
        start += rank
        first.append(lax.ppermute(part, "grid", [(i, ((i + 2 * d) % size) ^ 1) for i in range(size)]))
    return (first, mate_first), ([mate_swap(part) for part in first], from_mate)


def per_device(starts, coriolis):
    own = starts[0]
    _, rows, length = own.shape
    ranks, mate_rank, send_tables, apply_tables = y_tables(length, lax.axis_size("grid"))
    plan = Plan(rows, length, ranks, mate_rank)
    table = jnp.asarray(x_tables(length))
    def stage(kinds, states, moments, others=((), ()), sends=False, groups=((), ())):
        received = exchange(plan, *moments)
        grads = along_x(*states, table)
        results = []
        for at, kind in enumerate(kinds):
            more = others[at] if kind != "join" else (*others[at], results[0][0])
            operands = (states[at], grads[at], *received[at], turning, apply)
            results.append(stage_call(plan, kind, *operands, send if sends else None, more, groups[at]))
        if not sends:
            return results
        return *zip(*[r[:-1] for r in results]), [r[-1] for r in results]

    before = ahead_in_time(own, 1)
    both_send, both_apply = jnp.asarray(send_tables), jnp.asarray(apply_tables)
    opened = enter_call(plan, own, tables=(both_send, both_apply, coriolis[None, :]))
    states, moments, (send, apply, turning) = opened[0:4:2], list(opened[1:4:2]), opened[4:]
    states, moments = stage(("move", "move"), states, moments, sends=True)
    states, moments = stage(("move", "move"), states, moments, sends=True)
    (lead,) = stage(("lead",), states, moments, groups=(FAR,))
    far = [ahead_in_time(fields, 2) for fields in lead]

    before, _ = lax.optimization_barrier((before, lead[0]))
    entered = enter_call(plan, own, before, send=send)
    states, moments = entered[0::2], list(entered[1::2])
    nodes_one, rates_zero, moments = stage(("keep", "keep"), states, moments, sends=True)
    states, rates_one, moments = stage(("keep", "keep"), nodes_one, moments, sends=True)
    olds = list(zip(rates_zero, rates_one))
    theirs, mine = stage(("correct", "correct"), states, moments, olds, groups=((3,), NEAR))
    near = [ahead_in_time(fields, 1) for fields in mine[: len(NEAR)]]

    results = [
        restart_call(plan, far, theirs[:1], nodes_one[0], theirs[1], send),
        restart_call(plan, near, (), nodes_one[1], mine[-2], send),
    ]
    lasts = ((theirs[2],), (mine[-1],))
    ends = stage(("end", "join"), [r[0] for r in results], [r[1] for r in results], lasts)
    return ends[1][0][None]


def solution(mesh):
    return jax.shard_map(
        per_device,
        mesh=mesh,
        in_specs=(P("tm", None, "grid", None), P("grid")),
        out_specs=P("tm", None, "grid", None),
        check_vma=False,
    )
```

```python
import functools
import math

import jax
import jax.numpy as jnp
import ml_dtypes
import numpy as np
from jax import lax
from jax.experimental import pallas as pl
from jax.experimental.pallas import tpu as pltpu
from jax.sharding import PartitionSpec as P

SWEEPS = 2
STEP_LENGTH = 0.001
HALF_STEP = 0.5 * STEP_LENGTH
GRAVITY = 1.0
CORRECT_FIRST = (5.0 / 24.0 - 0.5, 8.0 / 24.0, -1.0 / 24.0)
CORRECT_SECOND = (-1.0 / 24.0, 8.0 / 24.0 - 0.5, 5.0 / 24.0)
TOLERANCE = 1e-8
ROWS = 8
KERNEL_BYTES = 8 * 2**20
KERNEL_FLOPS = 10**10
FAR = (3,)
NEAR = (3,)
F32 = jnp.float32
BF16 = jnp.bfloat16


def kernel_values(length):
    values = np.zeros(length)
    for j in range(1, length):
        values[j] = (0.5 if j % 2 == 0 else -0.5) / math.tan(math.pi * j / length)
    values[length // 2] = 0.0
    return values


def toeplitz(values, rows, cols, offset):
    index = np.arange(rows)[:, None] - np.arange(cols)[None, :] + offset
    return values[index % len(values)]


def cross_factors(block, tolerance):
    rest = block.copy()
    lefts, rights = [], []
    while True:
        at = int(np.argmax(np.abs(rest)))
        i, j = divmod(at, rest.shape[1])
        pivot = rest[i, j]
        small = abs(pivot) <= tolerance
        if (small and lefts and len(lefts) % 8 == 0) or len(lefts) == block.shape[0]:
            break
        if abs(pivot) == 0.0:
            left, right = np.zeros(rest.shape[0]), np.zeros(rest.shape[1])
        else:
            left, right = rest[:, j] / pivot, rest[i, :].copy()
        lefts.append(left)
        rights.append(right)
        rest = rest - left[:, None] * right[None, :]
    return np.stack(lefts, axis=1), np.stack(rights, axis=0)


def two_parts(table):
    high = table.astype(ml_dtypes.bfloat16)
    low = (table - high.astype(np.float64)).astype(ml_dtypes.bfloat16)
    return high, low


def pad_rows(table, multiple):
    extra = -table.shape[0] % multiple
    return np.pad(table, ((0, extra), (0, 0)))


def x_tables(length):
    values = kernel_values(length)
    half = length // 2
    near = toeplitz(values, half, half, 0).T
    far = toeplitz(values, half, half, half).T
    plus = two_parts(0.5 * (near + far))
    minus = two_parts(0.5 * (near - far))
    return np.stack([plus[0], plus[1], minus[0], minus[1]])


@functools.lru_cache(maxsize=None)
def y_tables(length, devices):
    rows = length // devices
    pair = 2 * rows
    pairs = devices // 2
    values = kernel_values(length)
    tolerance = TOLERANCE * float(np.max(np.abs(values)))
    factors = [cross_factors(toeplitz(values, pair, pair, d * pair), tolerance) for d in range(1, pairs)]
    ranks = tuple(f[0].shape[1] for f in factors)
    mates = [cross_factors(toeplitz(values, rows, rows, rows if k == 0 else -rows), tolerance) for k in range(2)]
    mate_rank = max(m[0].shape[1] for m in mates)
    send, apply = [], []
    for k in range(2):
        span = slice(k * rows, (k + 1) * rows)
        to_mate = np.pad(mates[k][1], ((0, mate_rank - mates[k][1].shape[0]), (0, 0)))
        from_mate = np.pad(mates[1 - k][0], ((0, 0), (0, mate_rank - mates[1 - k][0].shape[1])))
        down = pad_rows(np.concatenate([f[1][:, span] for f in factors] + [to_mate], axis=0), 16)
        send.append(np.concatenate(two_parts(down), axis=0))
        own = pad_rows(toeplitz(values, rows, rows, 0).T, 16).T
        up = np.concatenate([own] + [f[0][span] for f in factors] + [from_mate], axis=1)
        up = pad_rows(up.T, 16).T
        apply.append(np.concatenate(two_parts(up), axis=0))
    return ranks, mate_rank, np.stack(send), np.stack(apply)


COST = pl.CostEstimate(flops=KERNEL_FLOPS, transcendentals=0, bytes_accessed=2**20)


def parts_of(value):
    high = value.astype(BF16)
    return high, (value - high.astype(F32)).astype(BF16)


def dot(left, right):
    return jnp.dot(left, right, preferred_element_type=F32)


def product(stacked, high, low):
    count = stacked.shape[0] // 2
    both = dot(stacked, high)
    return both[:count] + both[count:] + dot(stacked[:count], low)


VMEM = pl.BlockSpec(memory_space=pltpu.VMEM)
HBM = pl.BlockSpec(memory_space=pltpu.HBM)


def on_chip_call(body, operands, shapes, keep=True, **options):
    held = [pltpu.with_memory_space_constraint(a, pltpu.VMEM) for a in operands]
    outs = [pltpu.VMEM(s.shape, s.dtype) for s in shapes] if keep else shapes
    return pl.pallas_call(
        body,
        in_specs=[VMEM] * len(held),
        out_specs=[VMEM if keep else HBM] * len(outs),
        out_shape=outs,
        compiler_params=pltpu.CompilerParams(vmem_limit_bytes=KERNEL_BYTES),
        cost_estimate=COST,
        **options,
    )(*held)


def x_kernel(theirs_ref, mine_ref, table_ref, grad_theirs_ref, grad_mine_ref):
    theirs, mine = theirs_ref[...], mine_ref[...]

    def folded(total, at):
        high, low = parts_of(total)
        return dot(high, table_ref[at]) + dot(low, table_ref[at]) + dot(high, table_ref[at + 1])

    even = folded(mine + theirs, 0)
    odd = folded(mine - theirs, 2)
    grad_mine_ref[...] = even + odd
    grad_theirs_ref[...] = even - odd


def along_x(theirs, mine, table):
    fields, rows, half = mine.shape
    flat = [a.reshape(fields * rows, half) for a in (theirs, mine)]
    shape = jax.ShapeDtypeStruct(flat[0].shape, F32)
    grads = on_chip_call(x_kernel, [*flat, table], [shape, shape], name="along_x")
    return [g.reshape(mine.shape) for g in grads]


def member_of_pair():
    return lax.rem(lax.axis_index("grid"), 2)


class Plan:
    def __init__(self, rows, length, ranks, mate_rank):
        self.rows, self.length, self.half = rows, length, length // 2
        self.ranks, self.mate_rank, self.total = ranks, mate_rank, sum(ranks)
        self.state = jax.ShapeDtypeStruct((3, rows, self.half), F32)
        self.whole = jax.ShapeDtypeStruct((3, rows, length), F32)
        self.moments = [jax.ShapeDtypeStruct((3, self.total + mate_rank, self.half), F32)]

    def columns(self, mine):
        at = member_of_pair() if mine else 1 - member_of_pair()
        return pl.ds(pl.multiple_of(at * self.half, 128), self.half)

    def emit_moments(self, next_ref, send_ref, moments_ref):
        for f in range(3):
            found = product(send_ref[...], *parts_of(next_ref[f]))
            moments_ref[f] = found[: self.total + self.mate_rank]

    def y_gradient(self, f, state_ref, pair_refs, mate_ref, apply_ref):
        pieces = [state_ref[f]]
        if self.rows % 16:
            pieces.append(jnp.zeros((-self.rows % 16, self.half), F32))
        pieces += [ref[f] for ref in pair_refs]
        pieces.append(mate_ref[f, mate_ref.shape[1] - self.mate_rank :])
        width = apply_ref.shape[1] - sum(p.shape[0] for p in pieces)
        if width:
            pieces.append(jnp.zeros((width, self.half), F32))
        return product(apply_ref[...], *parts_of(jnp.concatenate(pieces, axis=0)))


def tendency_rows(h, u, v, gx, gy, turning):
    rate_h = -(u * gx[0] + v * gy[0]) - (1.0 + h) * (gx[1] + gy[2])
    rate_u = -(u * gx[1] + v * gy[1]) + turning * v - GRAVITY * gx[0]
    rate_v = -(u * gx[2] + v * gy[2]) - turning * u - GRAVITY * gy[0]
    return rate_h, rate_u, rate_v


def enter_call(plan, state, received=None, tables=None, send=None, halves=(0, 1)):
    sources = [state] if received is None else [state, received]
    opening, count = tables is not None, len(halves)
    held_in = pltpu.HBM if opening else pltpu.VMEM
    more = [pltpu.with_memory_space_constraint(a, held_in) for a in (tables if opening else [send])]

    def body(*refs):
        source_refs, refs = refs[: len(sources)], refs[len(sources) :]
        more_refs, outs = refs[: len(more)], refs[len(more) :]
        nexts, moments, arrived = outs[0 : 2 * count : 2], outs[1 : 2 * count : 2], outs[-1]

        def copy(source_ref, at):
            return pltpu.make_async_copy(source_ref.at[:, :, plan.columns(halves[at] == 1)], nexts[at], arrived.at[at])

        def start(source_ref):
            for at in range(count):
                copy(source_ref, at).start()

        if opening:
            picks = [
                pltpu.make_async_copy(more_refs[n].at[member_of_pair()], outs[2 * count + n], arrived.at[2 + n]) for n in range(2)
            ]
            picks.append(pltpu.make_async_copy(more_refs[2], outs[-2], arrived.at[4]))
            for pick in picks:
                pick.start()
            start(source_refs[0])
            for pick in picks:
                pick.wait()
            square = (plan.rows, plan.rows)
            here = lax.broadcasted_iota(jnp.int32, square, 0) == lax.broadcasted_iota(jnp.int32, square, 1)
            outs[2 * count + 2][...] = jnp.sum(jnp.where(here, outs[-2][...], 0.0), axis=1, keepdims=True)
        elif received is None:
            start(source_refs[0])
        else:
            first = lax.axis_index("tm") == 0
            pl.when(first)(lambda: start(source_refs[0]))
            pl.when(jnp.logical_not(first))(lambda: start(source_refs[1]))
        send_ref = outs[2 * count] if opening else more_refs[0]
        for at in range(count):
            copy(source_refs[0], at).wait()
            plan.emit_moments(nexts[at], send_ref, moments[at])

    shapes = [plan.state, *plan.moments] * count
    scratch = [pltpu.SemaphoreType.DMA((5,))]
    if opening:
        shapes += [jax.ShapeDtypeStruct(a.shape[1:], a.dtype) for a in tables[:2]]
        shapes.append(jax.ShapeDtypeStruct((plan.rows, 1), F32))
        scratch.insert(0, pltpu.VMEM((1, plan.rows), F32))
    return pl.pallas_call(
        body,
        in_specs=[HBM] * len(sources) + [HBM if opening else VMEM] * len(more),
        out_specs=[VMEM] * len(shapes),
        out_shape=[pltpu.VMEM(s.shape, s.dtype) for s in shapes],
        scratch_shapes=scratch,
        compiler_params=pltpu.CompilerParams(vmem_limit_bytes=KERNEL_BYTES),
        cost_estimate=COST,
        name="enter",
    )(*sources, *more)


def field_of(refs, f):
    for ref in refs:
        if f < ref.shape[0]:
            return ref[f]
        f -= ref.shape[0]


def restart_call(plan, received, second, node_one, added, send):
    count = len(received)

    def body(*refs):
        received_refs, (node_ref, added_ref, *rest) = refs[:count], refs[count:]
        second_refs, (send_ref, next_ref, moments_ref) = rest[: len(second)], rest[len(second) :]
        for f in range(3):
            value = field_of(received_refs, f)
            if second:
                value = jnp.where(lax.axis_index("tm") == 1, field_of(second_refs, f), value)
            next_ref[f] = jnp.where(lax.axis_index("tm") == 0, node_ref[f], value) + added_ref[f]
        plan.emit_moments(next_ref, send_ref, moments_ref)

    operands = [*received, node_one, added, *second, send]
    return on_chip_call(body, operands, [plan.state, *plan.moments], name="restart")


def stage_call(plan, kind, state, grad_x, pair_in, mate_in, turning, apply, send=None, others=(), groups=()):
    count = len(pair_in)
    join = kind == "join"

    def body(state_ref, grad_ref, turning_ref, *rest):
        pair_refs, (mate_ref, apply_ref), rest = rest[:count], rest[count : count + 2], rest[count + 2 :]
        other_refs, rest = rest[: len(others)], rest[len(others) :]
        if send is not None:
            send_ref, rest = rest[0], rest[1:]
        leads, outs, grad_y = rest[: len(groups)], rest[len(groups) : len(shapes)], rest[len(shapes)]
        if join:
            made_ref, done = rest[len(shapes) + 1 :]
            whole_ref, outs = outs[0], [made_ref]
            copies = [
                pltpu.make_async_copy(ref, whole_ref.at[:, :, plan.columns(at == 1)], done.at[at])
                for at, ref in enumerate((other_refs[1], made_ref))
            ]
            copies[0].start()
        for f in range(3):
            grad_y[f] = plan.y_gradient(f, state_ref, pair_refs, mate_ref, apply_ref)
        for start in range(0, plan.rows, ROWS):
            at = slice(start, start + ROWS)
            now = [state_ref[f, at] for f in range(3)]
            rates = tendency_rows(
                *now, [grad_ref[f, at] for f in range(3)], [grad_y[f, at] for f in range(3)], turning_ref[at]
            )
            for f in range(3):
                ahead = now[f] + HALF_STEP * rates[f]
                if groups:
                    group = next(g for g in range(len(groups)) if f < sum(groups[: g + 1]))
                    leads[group][f - sum(groups[:group]), at] = ahead
                elif kind in ("end", "join"):
                    outs[0][f, at] = ahead + other_refs[0][f, at]
                else:
                    outs[0][f, at] = ahead
                if kind == "keep":
                    outs[1][f, at] = rates[f]
                if kind == "correct":
                    olds = (other_refs[0][f, at], other_refs[1][f, at], rates[f])
                    for out, weights in zip(outs, (CORRECT_FIRST, CORRECT_SECOND)):
                        out[f, at] = sum((STEP_LENGTH * w) * r for w, r in zip(weights, olds))
        if send is not None:
            plan.emit_moments(outs[0], send_ref, outs[-1])
        if join:
            copies[1].start()
            for copy in copies:
                copy.wait()

    operands = [state, grad_x, turning, *pair_in, mate_in, apply, *others]
    shapes = [jax.ShapeDtypeStruct((g, *plan.state.shape[1:]), F32) for g in groups]
    shapes += [plan.state] * {"move": 1, "keep": 2, "lead": 0, "correct": 2, "end": 1, "join": 0}[kind]
    scratch = [pltpu.VMEM(plan.state.shape, F32)]
    if send is not None:
        operands.append(send)
        shapes += plan.moments
    if join:
        shapes = [plan.whole]
        scratch += [pltpu.VMEM(plan.state.shape, F32), pltpu.SemaphoreType.DMA((2,))]
    return on_chip_call(body, operands, shapes, keep=not join, scratch_shapes=scratch, name=f"stage_{kind}")


def ahead_in_time(array, by):
    size = lax.axis_size("tm")
    return lax.ppermute(array, "tm", [(i, i + by) for i in range(size - by)])


def mate_swap(array):
    size = lax.axis_size("grid")
    return lax.ppermute(array, "grid", [(i, i ^ 1) for i in range(size)])


def exchange(plan, theirs, mine):
    size = lax.axis_size("grid")
    from_mate = mate_swap(theirs)
    mate_first = mate_swap(mine[:, plan.total :])
    merged = mine[:, : plan.total] + from_mate[:, : plan.total]
    first, start = [], 0
    for d, rank in enumerate(plan.ranks, 1):
        part = merged[:, start : start + rank]
        start += rank
        first.append(lax.ppermute(part, "grid", [(i, ((i + 2 * d) % size) ^ 1) for i in range(size)]))
    return (first, mate_first), ([mate_swap(part) for part in first], from_mate)


def per_device(starts, coriolis):
    own = starts[0]
    _, rows, length = own.shape
    ranks, mate_rank, send_tables, apply_tables = y_tables(length, lax.axis_size("grid"))
    plan = Plan(rows, length, ranks, mate_rank)
    table = jnp.asarray(x_tables(length))
    def stage(kinds, states, moments, others=((), ()), sends=False, groups=((), ())):
        received = exchange(plan, *moments)
        grads = along_x(*states, table)
        results = []
        for at, kind in enumerate(kinds):
            more = others[at] if kind != "join" else (*others[at], results[0][0])
            operands = (states[at], grads[at], *received[at], turning, apply)
            results.append(stage_call(plan, kind, *operands, send if sends else None, more, groups[at]))
        if not sends:
            return results
        return *zip(*[r[:-1] for r in results]), [r[-1] for r in results]

    before = ahead_in_time(own, 1)
    both_send, both_apply = jnp.asarray(send_tables), jnp.asarray(apply_tables)
    opened = enter_call(plan, own, tables=(both_send, both_apply, coriolis[None, :]), halves=(0,))
    send, apply, turning = opened[2:]
    opened_mine = enter_call(plan, own, send=send, halves=(1,))
    states, moments = [opened[0], opened_mine[0]], [opened[1], opened_mine[1]]
    states, moments = stage(("move", "move"), states, moments, sends=True)
    states, moments = stage(("move", "move"), states, moments, sends=True)
    (lead,) = stage(("lead",), states, moments, groups=(FAR,))
    far = [ahead_in_time(fields, 2) for fields in lead]

    before, _ = lax.optimization_barrier((before, lead[0]))
    entered = enter_call(plan, own, before, send=send)
    states, moments = entered[0::2], list(entered[1::2])
    nodes_one, rates_zero, moments = stage(("keep", "keep"), states, moments, sends=True)
    states, rates_one, moments = stage(("keep", "keep"), nodes_one, moments, sends=True)
    olds = list(zip(rates_zero, rates_one))
    theirs, mine = stage(("correct", "correct"), states, moments, olds, groups=((3,), NEAR))
    near = [ahead_in_time(fields, 1) for fields in mine[: len(NEAR)]]

    results = [
        restart_call(plan, far, theirs[:1], nodes_one[0], theirs[1], send),
        restart_call(plan, near, (), nodes_one[1], mine[-2], send),
    ]
    lasts = ((theirs[2],), (mine[-1],))
    ends = stage(("end", "join"), [r[0] for r in results], [r[1] for r in results], lasts)
    return ends[1][0][None]


def solution(mesh):
    return jax.shard_map(
        per_device,
        mesh=mesh,
        in_specs=(P("tm", None, "grid", None), P("grid")),
        out_specs=P("tm", None, "grid", None),
        check_vma=False,
    )
```
